256 devices in a mesh: row: 16 (over z, core), col: 16 (over x, y).
Axes of the slice: x: 4, y: 4, z: 8, core: 2. Of those that a mesh axis runs over, the one named last changes fastest.
Arguments:
- gen_showers: bfloat16 [16384, 6480], P(('row', 'col')), may hold values from -10 to 10
- ref_showers: bfloat16 [16384, 6480], P(('row', 'col')), may hold values from -10 to 10
- w_in: bfloat16 [6480, 512], replicated, may hold values from -0.078125 to 0.078125
- b_in: float32 [512], replicated, may hold values from -4 to 4
- w_out: bfloat16 [512, 256], replicated, may hold values from -0.25 to 0.25
Outputs:
- gen_potential: float32 [16384], P('row')
- ref_potential: float32 [16, 1024], P(None, 'col')
The draws below stay inside these ranges and needn't reach their ends.
All inputs are finite; a program needn't handle non-finite values.
Results may differ from the reference program's by a relative error of at most 0.0003.
Values sent between devices are 32-bit elements; how exact they have to be, the bound alone decides.
A program may use at most 128 MiB of HBM per device.

```python
import math
import jax
import jax.numpy as jnp
from jax import lax

VOXELS = 6480
UNITS = 512
FEAT = 256
ROWS_DEV = 64
ITERS = 3
N_SHOW = 16384
GEN_BLOCK = 1024
REF_BLOCK = 1024
N_ROW = 16
N_COL = 16


def shower_values(key):
    base = jnp.clip(jax.random.normal(key, (N_SHOW, VOXELS), jnp.float32), -6.0, 6.0)
    flags = jax.random.randint(jax.random.fold_in(key, 7), (N_SHOW, 1), 0, 16) == 0
    picked = jax.random.randint(jax.random.fold_in(key, 8), (), 0, N_SHOW)
    flags = jnp.logical_or(flags, jnp.arange(N_SHOW)[:, None] == picked)
    strength = jax.random.uniform(jax.random.fold_in(key, 9), (N_SHOW, 1), jnp.float32, 4.0, 10.0)
    magnitude = jax.random.uniform(jax.random.fold_in(key, 10), (N_SHOW, VOXELS), jnp.float32, 0.6, 1.0) * strength
    signs = 2.0 * jax.random.randint(jax.random.fold_in(key, 11), (N_SHOW, VOXELS), 0, 2).astype(jnp.float32) - 1.0
    return jnp.where(flags, signs * magnitude, base)


def draw_gen_showers(key, part):
    return shower_values(jax.random.fold_in(key, 101)).astype(jnp.bfloat16)


def draw_ref_showers(key, part):
    return shower_values(jax.random.fold_in(key, 202)).astype(jnp.bfloat16)


def scatter_about(key, extent, deviation, limit, dtype=jnp.bfloat16):
    return jnp.clip(deviation * jax.random.normal(key, extent, jnp.float32), -limit, limit).astype(dtype)


def setup_inputs(seed: int = 0) -> dict:
    keys = jax.random.split(jax.random.key(seed), 6)
    gen_showers = draw_gen_showers(jax.random.fold_in(keys[5], 71), 0)
    ref_showers = draw_ref_showers(jax.random.fold_in(keys[5], 71), 0)
    w_in = scatter_about(keys[2], (VOXELS, UNITS), VOXELS ** -0.5, 0.078125)
    b_in = scatter_about(keys[3], (UNITS,), 1.0, 4.0, jnp.float32)
    w_out = scatter_about(keys[4], (UNITS, FEAT), UNITS ** -0.5, 0.25)
    return {"gen_showers": gen_showers, "ref_showers": ref_showers, "w_in": w_in, "b_in": b_in, "w_out": w_out}


EPSILON = 0.1


def embed(showers, w_in, b_in, w_out):
    hidden = jnp.dot(showers, w_in, preferred_element_type=jnp.float32) + b_in
    hidden = jnp.maximum(hidden, 0.0)
    features = jnp.dot(hidden, w_out.astype(jnp.float32), precision=lax.Precision.HIGHEST)
    squares = jnp.sum(jnp.square(features), axis=1)
    return features, squares


def soft_minimum(near_feat, near_sq, far_feat, far_sq, far_pot, block_size):
    block_count = near_feat.shape[0] // block_size
    log_weight = -math.log(far_feat.shape[0])
    far_trans = far_feat.T

    def one_block(pieces):
        feat_block, sq_block = pieces
        inner_prod = jnp.dot(feat_block, far_trans, precision=lax.Precision.HIGHEST)
        tile_cost = (sq_block[:, None] + far_sq[None, :] - 2.0 * inner_prod) / FEAT
        scaled = log_weight + (far_pot[None, :] - tile_cost) / EPSILON
        largest = jnp.max(scaled, axis=1)
        totals = jnp.sum(jnp.exp(scaled - largest[:, None]), axis=1)
        return -EPSILON * (largest + jnp.log(totals))

    result = lax.map(one_block, (near_feat.reshape(block_count, block_size, -1), near_sq.reshape(block_count, block_size)))
    return result.reshape(-1)


def reference(gen_showers, ref_showers, w_in, b_in, w_out):
    gen_feat, gen_sq = embed(gen_showers, w_in, b_in, w_out)
    ref_feat, ref_sq = embed(ref_showers, w_in, b_in, w_out)
    ref_pot = jnp.zeros((N_SHOW,), jnp.float32)
    gen_pot = jnp.zeros((N_SHOW,), jnp.float32)
    for sweep_idx in range(ITERS):
        gen_pot = soft_minimum(gen_feat, gen_sq, ref_feat, ref_sq, ref_pot, GEN_BLOCK)
        ref_pot = soft_minimum(ref_feat, ref_sq, gen_feat, gen_sq, gen_pot, REF_BLOCK)
    return gen_pot, ref_pot.reshape(N_ROW, N_COL * ROWS_DEV)
```

```python
import functools
import math

import jax
import jax.numpy as jnp
from jax import lax
from jax.experimental import pallas as pl
from jax.experimental.pallas import tpu as pltpu
from jax.sharding import PartitionSpec as P

EPSILON = 0.1
MESH = pl.DeviceIdType.MESH
F32 = jnp.float32
BF16 = jnp.bfloat16
LANES = 128
K_CHUNK = 1280


def split2(v):
    hi = v.astype(BF16)
    lo = (v - hi.astype(F32)).astype(BF16)
    return hi, lo


def mm(a, b):
    return jnp.dot(a, b, preferred_element_type=F32)


def kernel(
    n_row,
    n_col,
    gx,
    rx,
    w,
    b,
    wo,
    g_out,
    f_out,
    x_v,
    w_v,
    b_v,
    wo_v,
    gf,
    rf,
    g_hi,
    g_lo,
    r_hi,
    r_lo,
    tile,
    part,
    part2,
    colv,
    sqg,
    sqr,
    send1,
    recv1g,
    recv1f,
    send2,
    recv2,
    x_sem,
    w_sem,
    s_sem,
    gsend,
    grecv,
    esend,
    erecv,
):
    my_r = lax.axis_index("row")
    my_c = lax.axis_index("col")
    per = gx.shape[0]
    vox = gx.shape[1]
    feat = wo.shape[1]
    rows = per * n_col
    cols = per * n_row
    rq = rows // LANES
    cq = cols // LANES
    total = n_row * n_col * per
    kappa = 1.0 / (EPSILON * math.log(2.0))
    log2w = -math.log2(total)

    def row_peer(d):
        return (lax.rem(my_r + d, n_row), my_c)

    def col_peer(d):
        return (my_r, lax.rem(my_c + d, n_col))

    loads = [
        pltpu.make_async_copy(gx, x_v.at[pl.ds(0, per)], x_sem.at[0]),
        pltpu.make_async_copy(rx, x_v.at[pl.ds(per, per)], x_sem.at[1]),
        pltpu.make_async_copy(b, b_v, s_sem.at[0]),
        pltpu.make_async_copy(wo, wo_v, s_sem.at[1]),
    ]
    bounds = list(range(0, vox, K_CHUNK)) + [vox]
    if bounds[-1] - bounds[-2] < K_CHUNK // 2 and len(bounds) > 2:
        del bounds[-2]
    spans = list(zip(bounds[:-1], bounds[1:]))
    wloads = [
        pltpu.make_async_copy(w.at[pl.ds(k0, k1 - k0)], w_v.at[pl.ds(k0, k1 - k0)], w_sem.at[n])
        for n, (k0, k1) in enumerate(spans)
    ]
    loads[0].start()
    loads[1].start()
    for cp in wloads:
        cp.start()
    loads[2].start()
    loads[3].start()

    barrier = pltpu.get_barrier_semaphore()
    for d in range(1, n_row):
        pl.semaphore_signal(barrier, inc=1, device_id=row_peer(d), device_id_type=MESH)
    for d in range(1, n_col):
        pl.semaphore_signal(barrier, inc=1, device_id=col_peer(d), device_id_type=MESH)

    loads[0].wait()
    loads[1].wait()
    acc = None
    for n, (k0, k1) in enumerate(spans):
        wloads[n].wait()
        t = mm(x_v[:, k0:k1], w_v[k0:k1, :])
        acc = t if acc is None else acc + t
    loads[2].wait()
    loads[3].wait()
    hidden = jnp.maximum(acc + b_v[...], 0.0)
    h0 = hidden.astype(BF16)
    h1f = hidden - h0.astype(F32)
    h1 = h1f.astype(BF16)
    h2 = (h1f - h1.astype(F32)).astype(BF16)
    wov = wo_v[...]
    feats = mm(h0, wov) + (mm(h1, wov) + mm(h2, wov))
    gf[my_c] = feats[:per]
    rf[my_r] = feats[per:]

    pl.semaphore_wait(barrier, n_row + n_col - 2)

    gather = []
    for d in range(1, n_row):
        gather.append(
            pltpu.make_async_remote_copy(
                rf.at[my_r], rf.at[my_r], gsend.at[0], grecv.at[0], device_id=row_peer(d), device_id_type=MESH
            )
        )
    for d in range(1, n_col):
        gather.append(
            pltpu.make_async_remote_copy(
                gf.at[my_c], gf.at[my_c], gsend.at[1], grecv.at[1], device_id=col_peer(d), device_id_type=MESH
            )
        )
    for cp in gather:
        cp.start()

    def all_bytes(ref, count, sem):
        view = ref.at[pl.ds(0, count)]
        return pltpu.make_async_copy(view, view, sem)

    all_bytes(rf, n_row - 1, grecv.at[0]).wait()
    all_bytes(gf, n_col - 1, grecv.at[1]).wait()

    scale = 2.0 * kappa / feat
    half = cq

    for q in range(rq):
        per_q = LANES // per
        v = jnp.concatenate([gf[q * per_q + k] for k in range(per_q)], axis=0)
        hi, lo = split2(v * scale)
        g_hi[pl.ds(q * LANES, LANES), :] = hi
        g_lo[pl.ds(q * LANES, LANES), :] = lo
    for q in range(cq):
        v = jnp.concatenate([rf[q], rf[q + half]], axis=0)
        vt = v.T
        sqr[pl.ds(q, 1), :] = jnp.sum(vt * vt, axis=0, keepdims=True) * (1.0 / feat)
        hi, lo = split2(vt)
        r_hi[:, pl.ds(q * LANES, LANES)] = hi
        r_lo[:, pl.ds(q * LANES, LANES)] = lo

    nt = 256

    def tile_step(n, _):
        off = pl.multiple_of(n * nt, nt)
        rh = r_hi[:, pl.ds(off, nt)]
        rl = r_lo[:, pl.ds(off, nt)]
        gh = g_hi[...]
        tile[:, pl.ds(off, nt)] = mm(gh, rh) + (mm(g_lo[...], rh) + mm(gh, rl))
        return 0

    lax.fori_loop(0, cols // nt, tile_step, 0)

    RB = 32

    def blocks(body):
        def step(n, _):
            body(pl.multiple_of(n * RB, RB))
            return 0

        lax.fori_loop(0, rows // RB, step, 0)

    def lane_groups(v):
        return [v[:, q * LANES : (q + 1) * LANES] for q in range(cq)]

    def to_dense(src, dst, row0, op):
        for q in range(rq):
            blk = src[pl.ds(q * LANES, LANES), :].T
            dst[pl.ds(row0 + q, 1), :] = op(blk, axis=0, keepdims=True)

    def to_col(x8):
        for q in range(rq):
            colv[pl.ds(q * LANES, LANES), :] = jnp.broadcast_to(x8[q : q + 1, :], (LANES, LANES)).T

    def wide(x8, n):
        return [jnp.broadcast_to(x8[q : q + 1, :], (n, LANES)) for q in range(cq)]

    def tree(op, vs):
        vs = list(vs)
        while len(vs) > 1:
            vs = [op(vs[k], vs[k + 1]) if k + 1 < len(vs) else vs[k] for k in range(0, len(vs), 2)]
        return vs[0]

    add = lambda p, q: p + q

    def exchange(n, src, dst, me, peer, count):
        dst[me] = src[...]
        cps = [
            pltpu.make_async_remote_copy(
                src, dst.at[me], esend.at[n], erecv.at[n], device_id=peer(d), device_id_type=MESH
            )
            for d in range(1, count)
        ]
        for cp in cps:
            cp.start()
        all_bytes(dst, count - 1, erecv.at[n]).wait()
        return cps

    sent = list(gather)

    phi0 = -kappa * sqr[...] + log2w
    ph = wide(phi0, RB)

    def gen_max(off):
        t = lane_groups(tile[pl.ds(off, RB), :])
        m = tree(jnp.maximum, [a + p for a, p in zip(t, ph)])
        part[pl.ds(off, RB), :] = jnp.broadcast_to(jnp.max(m, axis=1, keepdims=True), (RB, LANES))

    blocks(gen_max)

    def gen_sum(off):
        m = part[pl.ds(off, RB), :]
        t = lane_groups(tile[pl.ds(off, RB), :])
        part2[pl.ds(off, RB), :] = tree(add, [jnp.exp2((a + p) - m) for a, p in zip(t, ph)])

    blocks(gen_sum)
    to_dense(part, send1, 0, jnp.max)
    to_dense(part2, send1, rq, jnp.sum)
    sent += exchange(0, send1, recv1g, my_c, col_peer, n_col)

    def lse2(ref, count, q):
        ms = [ref[k, 0:q, :] for k in range(count)]
        m = tree(jnp.maximum, ms)
        s = tree(add, [ref[k, q:, :] * jnp.exp2(ms[k] - m) for k in range(count)])
        return m + jnp.log2(s)

    gamma = -lse2(recv1g, n_col, rq)
    to_col(gamma + log2w)

    def ref_max(n, ms):
        off = pl.multiple_of(n * RB, RB)
        c = colv[pl.ds(off, RB), :]
        out = []
        for q in range(cq):
            t = tile[pl.ds(off, RB), q * LANES : (q + 1) * LANES] + c
            tile[pl.ds(off, RB), q * LANES : (q + 1) * LANES] = t
            out.append(jnp.maximum(ms[q], tree(jnp.maximum, [t[8 * k : 8 * k + 8] for k in range(RB // 8)])))
        return tuple(out)

    low = jnp.full((8, LANES), -jnp.inf, F32)
    ms = lax.fori_loop(0, rows // RB, ref_max, tuple(low for _ in range(cq)))
    cm = [jnp.max(m, axis=0, keepdims=True) for m in ms]
    cmb = [jnp.broadcast_to(m, (RB, LANES)) for m in cm]

    def fold(v):
        return tree(add, [v[8 * k : 8 * k + 8] for k in range(RB // 8)])

    def ref_sum(n, ss):
        off = pl.multiple_of(n * RB, RB)
        out = []
        for q in range(cq):
            e = jnp.exp2(tile[pl.ds(off, RB), q * LANES : (q + 1) * LANES] - cmb[q])
            tile[pl.ds(off, RB), q * LANES : (q + 1) * LANES] = e
            out.append(ss[q] + fold(e))
        return tuple(out)

    zero = jnp.zeros((8, LANES), F32)
    ss = lax.fori_loop(0, rows // RB, ref_sum, tuple(zero for _ in range(cq)))
    for q in range(cq):
        send2[pl.ds(q, 1), :] = cm[q]
        send2[pl.ds(cq + q, 1), :] = jnp.sum(ss[q], axis=0, keepdims=True)
    sent += exchange(1, send2, recv1f, my_r, row_peer, n_row)
    phi = -lse2(recv1f, n_row, cq)
    w8 = jnp.exp2(send2[0:cq, :] + phi)

    def gen_pass(n, scale8):
        vw = wide(scale8, RB)

        def body(off):
            t = lane_groups(tile[pl.ds(off, RB), :])
            part[pl.ds(off, RB), :] = tree(add, [a * p for a, p in zip(t, vw)])

        blocks(body)
        src = send1.at[pl.ds(0, rq)] if n == 2 else send1.at[pl.ds(rq, rq)]
        to_dense(part, send1, 0 if n == 2 else rq, jnp.sum)
        cps = exchange(n, src, recv2.at[n - 2], my_c, col_peer, n_col)
        return tree(add, [recv2[n - 2, k] for k in range(n_col)]), cps

    def ref_pass(n, scale8):
        to_col(scale8)

        def step(k, ss):
            off = pl.multiple_of(k * RB, RB)
            c = colv[pl.ds(off, RB), :]
            return tuple(
                ss[q] + fold(tile[pl.ds(off, RB), q * LANES : (q + 1) * LANES] * c) for q in range(cq)
            )

        ss = lax.fori_loop(0, rows // RB, step, tuple(zero for _ in range(cq)))
        row0 = 0 if n == 3 else cq
        for q in range(cq):
            send2[pl.ds(row0 + q, 1), :] = w8[q : q + 1, :] * jnp.sum(ss[q], axis=0, keepdims=True)
        cps = exchange(n, send2.at[pl.ds(row0, cq)], recv2.at[n - 2], my_r, row_peer, n_row)
        return tree(add, [recv2[n - 2, k] for k in range(n_row)]), cps

    def drain(n, ref, count):
        all_bytes(ref, count, esend.at[n]).wait()

    drain(0, recv1g, n_col - 1)
    r, cps = gen_pass(2, w8)
    drain(1, recv1f, n_row - 1)
    c, cps = ref_pass(3, 1.0 / r)
    r, cps = gen_pass(4, w8 / c)
    for q in range(rq):
        per_q = LANES // per
        v = jnp.concatenate([gf[q * per_q + k] for k in range(per_q)], axis=0)
        v = v * v
        s = functools.reduce(add, [v[:, k * LANES : (k + 1) * LANES] for k in range(feat // LANES)])
        sqg[pl.ds(q, 1), :] = jnp.sum(s.T, axis=0, keepdims=True) * (1.0 / feat)
    g_out[...] = (gamma - jnp.log2(r)) * (1.0 / kappa) + sqg[...]
    c, cps = ref_pass(5, 1.0 / r)
    f = (phi - jnp.log2(c)) * (1.0 / kappa) + sqr[...]
    f_out[pl.ds(0, half), :] = f[:, :per]
    f_out[pl.ds(half, half), :] = f[:, per:]
    for n, count in ((2, n_col), (3, n_row), (4, n_col), (5, n_row)):
        drain(n, recv2.at[n - 2], count - 1)
    all_bytes(rf, n_row - 1, gsend.at[0]).wait()
    all_bytes(gf, n_col - 1, gsend.at[1]).wait()


def body(n_row, n_col, gx, rx, w, b, wo):
    per, vox = gx.shape
    units, feat = wo.shape
    rows, cols = per * n_col, per * n_row
    rq, cq = rows // LANES, cols // LANES
    hbm = pl.BlockSpec(memory_space=pl.ANY)
    vmem = pl.BlockSpec(memory_space=pltpu.VMEM)
    dma = pltpu.SemaphoreType.DMA
    n_chunks = max(1, vox // K_CHUNK + 1)
    g8, f2 = pl.pallas_call(
        functools.partial(kernel, n_row, n_col),
        out_shape=(jax.ShapeDtypeStruct((rq, LANES), F32), jax.ShapeDtypeStruct((n_row, per), F32)),
        in_specs=[hbm] * 5,
        out_specs=(vmem, vmem),
        scratch_shapes=[
            pltpu.VMEM((2 * per, vox), BF16),
            pltpu.VMEM((vox, units), BF16),
            pltpu.VMEM((1, units), F32),
            pltpu.VMEM((units, feat), BF16),
            pltpu.VMEM((n_col, per, feat), F32),
            pltpu.VMEM((n_row, per, feat), F32),
            pltpu.VMEM((rows, feat), BF16),
            pltpu.VMEM((rows, feat), BF16),
            pltpu.VMEM((feat, cols), BF16),
            pltpu.VMEM((feat, cols), BF16),
            pltpu.VMEM((rows, cols), F32),
            pltpu.VMEM((rows, LANES), F32),
            pltpu.VMEM((rows, LANES), F32),
            pltpu.VMEM((rows, LANES), F32),
            pltpu.VMEM((rq, LANES), F32),
            pltpu.VMEM((cq, LANES), F32),
            pltpu.VMEM((2 * rq, LANES), F32),
            pltpu.VMEM((n_col, 2 * rq, LANES), F32),
            pltpu.VMEM((n_row, 2 * cq, LANES), F32),
            pltpu.VMEM((2 * cq, LANES), F32),
            pltpu.VMEM((4, max(n_col, n_row), max(rq, cq), LANES), F32),
            dma((2,)),
            dma((n_chunks,)),
            dma((2,)),
            dma((2,)),
            dma((2,)),
            dma((6,)),
            dma((6,)),
        ],
        compiler_params=pltpu.CompilerParams(
            collective_id=0, has_side_effects=True, vmem_limit_bytes=60 * 1024 * 1024
        ),
    )(gx, rx, w, b.reshape(1, units), wo)
    return g8.reshape(rows), f2


def solution(mesh):
    n_row, n_col = mesh.shape["row"], mesh.shape["col"]
    return jax.shard_map(
        functools.partial(body, n_row, n_col),
        mesh=mesh,
        in_specs=(P(("row", "col"), None), P(("row", "col"), None), P(), P(), P()),
        out_specs=(P("row"), P(None, "col")),
        check_vma=False,
    )
```

```python
import functools
import math

import jax
import jax.numpy as jnp
from jax import lax
from jax.experimental import pallas as pl
from jax.experimental.pallas import tpu as pltpu
from jax.sharding import PartitionSpec as P

EPSILON = 0.1
MESH = pl.DeviceIdType.MESH
F32 = jnp.float32
BF16 = jnp.bfloat16
LANES = 128
K_CHUNK = 1280
CHUNKS = 2


def split2(v):
    hi = v.astype(BF16)
    lo = (v - hi.astype(F32)).astype(BF16)
    return hi, lo


def mm(a, b):
    return jnp.dot(a, b, preferred_element_type=F32)


def kernel(
    n_row,
    n_col,
    n_x,
    gx,
    rx,
    w,
    b,
    wo,
    g_out,
    f_out,
    x_v,
    w_v,
    b_v,
    wo_v,
    gf,
    rf,
    g_hi,
    g_lo,
    r_hi,
    r_lo,
    tile,
    part,
    part2,
    colv,
    sqg,
    sqr,
    send1,
    recv1g,
    recv1f,
    send2,
    recv2,
    x_sem,
    w_sem,
    s_sem,
    gsend,
    grecv,
    esend,
    erecv,
):
    my_r = lax.axis_index("row")
    my_c = lax.axis_index("col")
    per = gx.shape[0]
    vox = gx.shape[1]
    feat = wo.shape[1]
    rows = per * n_col
    cols = per * n_row
    rq = rows // LANES
    cq = cols // LANES
    total = n_row * n_col * per
    n_y = n_col // n_x
    n_a = n_b = n_x
    kappa = 1.0 / (EPSILON * math.log(2.0))
    log2w = -math.log2(total)

    def row_peer(d):
        return (lax.rem(my_r + d, n_row), my_c)

    def col_peer(d):
        return (my_r, lax.rem(my_c + d, n_col))

    loads = [
        pltpu.make_async_copy(gx, x_v.at[pl.ds(0, per)], x_sem.at[0]),
        pltpu.make_async_copy(rx, x_v.at[pl.ds(per, per)], x_sem.at[1]),
        pltpu.make_async_copy(b, b_v, s_sem.at[0]),
        pltpu.make_async_copy(wo, wo_v, s_sem.at[1]),
    ]
    bounds = list(range(0, vox, K_CHUNK)) + [vox]
    if bounds[-1] - bounds[-2] < K_CHUNK // 2 and len(bounds) > 2:
        del bounds[-2]
    spans = list(zip(bounds[:-1], bounds[1:]))
    wloads = [
        pltpu.make_async_copy(w.at[pl.ds(k0, k1 - k0)], w_v.at[pl.ds(k0, k1 - k0)], w_sem.at[n])
        for n, (k0, k1) in enumerate(spans)
    ]
    loads[0].start()
    loads[1].start()
    for cp in wloads:
        cp.start()
    loads[2].start()
    loads[3].start()

    core = lax.rem(my_r, 2)
    px = my_c // n_y
    py = lax.rem(my_c, n_y)

    def z_index(d):
        return lax.rem(my_r + 2 * d + 2 * n_row, n_row)

    def partner_of(r):
        return r + 1 - 2 * core

    def ab_index(da, db):
        dx = da + (db - da) * core
        dy = db + (da - db) * core
        return lax.rem(px + dx + 2 * n_x, n_x) * n_y + lax.rem(py + dy + 2 * n_y, n_y)

    n_z = n_row // 2
    zdev = {d % n_z: (z_index(d), my_c) for d in (1, -1, 2, -2) if d % n_z}
    adev = {d % n_a: (my_r, ab_index(d, 0)) for d in (1, -1, 2) if d % n_a}
    bdev = {d % n_b: (my_r, ab_index(0, d)) for d in (1, -1, 2) if d % n_b}
    pdev = (partner_of(my_r), my_c)
    near = [*zdev.values(), *adev.values(), *bdev.values(), pdev]
    barrier = pltpu.get_barrier_semaphore()
    for dev in near:
        pl.semaphore_signal(barrier, inc=1, device_id=dev, device_id_type=MESH)

    loads[0].wait()
    loads[1].wait()
    acc = None
    for n, (k0, k1) in enumerate(spans):
        wloads[n].wait()
        t = mm(x_v[:, k0:k1], w_v[k0:k1, :])
        acc = t if acc is None else acc + t
    loads[2].wait()
    loads[3].wait()
    hidden = jnp.maximum(acc + b_v[...], 0.0)
    h0 = hidden.astype(BF16)
    h1f = hidden - h0.astype(F32)
    h1 = h1f.astype(BF16)
    h2 = (h1f - h1.astype(F32)).astype(BF16)
    wov = wo_v[...]
    feats = mm(h0, wov) + (mm(h1, wov) + mm(h2, wov))
    gf[my_c] = feats[:per]
    rf[my_r] = feats[per:]

    pl.semaphore_wait(barrier, len(near))

    ch = per // CHUNKS

    def piece(ref, block, c):
        return ref.at[block, pl.ds(c * ch, ch)]

    def send(ref, block, c, dev, slot, which):
        pltpu.make_async_remote_copy(
            piece(ref, block, c),
            piece(ref, block, c),
            gsend.at[which],
            grecv.at[slot],
            device_id=dev,
            device_id_type=MESH,
        ).start()

    def arrived(ref, block, c, slot):
        v = piece(ref, block, c)
        pltpu.make_async_copy(v, v, grecv.at[slot]).wait()

    halves = {1: range(CHUNKS // 2), -1: range(CHUNKS // 2, CHUNKS)}

    def reach(n, c):
        out = []
        for s in (1, -1):
            far = n // 2 if c in halves[s] else (n - 1) // 2
            out += [(s, h) for h in range(1, far + 1)]
        return out

    order = []
    for c in range(CHUNKS):
        for s, h in reach(n_z, c):
            order.append((h if h <= 2 else h + 3, 1 if h <= 2 else 2, c, "z", s * h, 0))
        for sb, hb in reach(n_b, c):
            order.append((hb + 2, 1, c, "b", 0, sb * hb))
        for sa, ha in reach(n_a, c):
            order.append((ha, 1, c, "a", sa * ha, 0))
            for sb, hb in reach(n_b, c):
                order.append((ha + hb + 3, 2, c, "b", sa * ha, sb * hb))
    order.sort(key=lambda o: (o[0], o[2]))
    slots = {o[2:]: n for n, o in enumerate(order)}
    last = len(slots)

    def to_z(c, block, d, step):
        send(rf, block, c, zdev[step % n_z], slots[(c, "z", d, 0)], 0)

    def to_partner(block, c):
        send(rf, block, c, pdev, last, 0)

    def to_a(c, d):
        send(gf, my_c, c, adev[d % n_a], slots[(c, "a", d, 0)], 1)

    def to_b(c, a):
        for s, h in reach(n_b, c):
            send(gf, ab_index(-a, 0), c, bdev[s * h % n_b], slots[(c, "b", a, s * h)], 1)

    for c in range(CHUNKS):
        for s, h in sorted(reach(n_z, c), key=lambda o: -o[1]):
            if h <= 2:
                to_z(c, my_r, s * h, s * h)
        for s, h in reach(n_a, c):
            to_a(c, s * h)
    for c in range(CHUNKS):
        to_b(c, 0)
        to_partner(my_r, c)
    for _, _, c, kind, p, q in order:
        slot = slots[(c, kind, p, q)]
        if kind == "z":
            block = z_index(-p)
            arrived(rf, block, c, slot)
            s = 1 if p > 0 else -1
            if p * s == 2:
                for h in (4, 3):
                    if (s, h) in reach(n_z, c):
                        to_z(c, block, s * h, s * (h - 2))
            to_partner(block, c)
        elif p and not q:
            arrived(gf, ab_index(-p, 0), c, slot)
            to_b(c, p)
        else:
            arrived(gf, ab_index(-p, -q), c, slot)

    def all_bytes(ref, count, sem):
        view = ref.at[pl.ds(0, count)]
        return pltpu.make_async_copy(view, view, sem)

    all_bytes(rf, n_z, grecv.at[last]).wait()

    scale = 2.0 * kappa / feat
    half = cq

    for q in range(rq):
        per_q = LANES // per
        v = jnp.concatenate([gf[q * per_q + k] for k in range(per_q)], axis=0)
        hi, lo = split2(v * scale)
        g_hi[pl.ds(q * LANES, LANES), :] = hi
        g_lo[pl.ds(q * LANES, LANES), :] = lo
    for q in range(cq):
        v = jnp.concatenate([rf[q], rf[q + half]], axis=0)
        vt = v.T
        sqr[pl.ds(q, 1), :] = jnp.sum(vt * vt, axis=0, keepdims=True) * (1.0 / feat)
        hi, lo = split2(vt)
        r_hi[:, pl.ds(q * LANES, LANES)] = hi
        r_lo[:, pl.ds(q * LANES, LANES)] = lo

    nt = 256

    def tile_step(n, _):
        off = pl.multiple_of(n * nt, nt)
        rh = r_hi[:, pl.ds(off, nt)]
        rl = r_lo[:, pl.ds(off, nt)]
        gh = g_hi[...]
        tile[:, pl.ds(off, nt)] = mm(gh, rh) + (mm(g_lo[...], rh) + mm(gh, rl))
        return 0

    lax.fori_loop(0, cols // nt, tile_step, 0)

    RB = 32

    def blocks(body):
        def step(n, _):
            body(pl.multiple_of(n * RB, RB))
            return 0

        lax.fori_loop(0, rows // RB, step, 0)

    def lane_groups(v):
        return [v[:, q * LANES : (q + 1) * LANES] for q in range(cq)]

    def to_dense(src, dst, row0, op):
        for q in range(rq):
            blk = src[pl.ds(q * LANES, LANES), :].T
            dst[pl.ds(row0 + q, 1), :] = op(blk, axis=0, keepdims=True)

    def to_col(x8):
        for q in range(rq):
            colv[pl.ds(q * LANES, LANES), :] = jnp.broadcast_to(x8[q : q + 1, :], (LANES, LANES)).T

    def wide(x8, n):
        return [jnp.broadcast_to(x8[q : q + 1, :], (n, LANES)) for q in range(cq)]

    def tree(op, vs):
        vs = list(vs)
        while len(vs) > 1:
            vs = [op(vs[k], vs[k + 1]) if k + 1 < len(vs) else vs[k] for k in range(0, len(vs), 2)]
        return vs[0]

    add = lambda p, q: p + q

    def exchange(n, src, dst, me, peer, count):
        dst[me] = src[...]
        cps = [
            pltpu.make_async_remote_copy(
                src, dst.at[me], esend.at[n], erecv.at[n], device_id=peer(d), device_id_type=MESH
            )
            for d in range(1, count)
        ]
        for cp in cps:
            cp.start()
        all_bytes(dst, count - 1, erecv.at[n]).wait()
        return cps

    sent = []

    phi0 = -kappa * sqr[...] + log2w
    ph = wide(phi0, RB)

    def gen_max(off):
        t = lane_groups(tile[pl.ds(off, RB), :])
        m = tree(jnp.maximum, [a + p for a, p in zip(t, ph)])
        part[pl.ds(off, RB), :] = jnp.broadcast_to(jnp.max(m, axis=1, keepdims=True), (RB, LANES))

    blocks(gen_max)

    def gen_sum(off):
        m = part[pl.ds(off, RB), :]
        t = lane_groups(tile[pl.ds(off, RB), :])
        part2[pl.ds(off, RB), :] = tree(add, [jnp.exp2((a + p) - m) for a, p in zip(t, ph)])

    blocks(gen_sum)
    to_dense(part, send1, 0, jnp.max)
    to_dense(part2, send1, rq, jnp.sum)
    sent += exchange(0, send1, recv1g, my_c, col_peer, n_col)

    def lse2(ref, count, q):
        ms = [ref[k, 0:q, :] for k in range(count)]
        m = tree(jnp.maximum, ms)
        s = tree(add, [ref[k, q:, :] * jnp.exp2(ms[k] - m) for k in range(count)])
        return m + jnp.log2(s)

    gamma = -lse2(recv1g, n_col, rq)
    to_col(gamma + log2w)

    def ref_max(n, ms):
        off = pl.multiple_of(n * RB, RB)
        c = colv[pl.ds(off, RB), :]
        out = []
        for q in range(cq):
            t = tile[pl.ds(off, RB), q * LANES : (q + 1) * LANES] + c
            tile[pl.ds(off, RB), q * LANES : (q + 1) * LANES] = t
            out.append(jnp.maximum(ms[q], tree(jnp.maximum, [t[8 * k : 8 * k + 8] for k in range(RB // 8)])))
        return tuple(out)

    low = jnp.full((8, LANES), -jnp.inf, F32)
    ms = lax.fori_loop(0, rows // RB, ref_max, tuple(low for _ in range(cq)))
    cm = [jnp.max(m, axis=0, keepdims=True) for m in ms]
    cmb = [jnp.broadcast_to(m, (RB, LANES)) for m in cm]

    def fold(v):
        return tree(add, [v[8 * k : 8 * k + 8] for k in range(RB // 8)])

    def ref_sum(n, ss):
        off = pl.multiple_of(n * RB, RB)
        out = []
        for q in range(cq):
            e = jnp.exp2(tile[pl.ds(off, RB), q * LANES : (q + 1) * LANES] - cmb[q])
            tile[pl.ds(off, RB), q * LANES : (q + 1) * LANES] = e
            out.append(ss[q] + fold(e))
        return tuple(out)

    zero = jnp.zeros((8, LANES), F32)
    ss = lax.fori_loop(0, rows // RB, ref_sum, tuple(zero for _ in range(cq)))
    for q in range(cq):
        send2[pl.ds(q, 1), :] = cm[q]
        send2[pl.ds(cq + q, 1), :] = jnp.sum(ss[q], axis=0, keepdims=True)
    sent += exchange(1, send2, recv1f, my_r, row_peer, n_row)
    phi = -lse2(recv1f, n_row, cq)
    w8 = jnp.exp2(send2[0:cq, :] + phi)

    def gen_pass(n, scale8):
        vw = wide(scale8, RB)

        def body(off):
            t = lane_groups(tile[pl.ds(off, RB), :])
            part[pl.ds(off, RB), :] = tree(add, [a * p for a, p in zip(t, vw)])

        blocks(body)
        src = send1.at[pl.ds(0, rq)] if n == 2 else send1.at[pl.ds(rq, rq)]
        to_dense(part, send1, 0 if n == 2 else rq, jnp.sum)
        cps = exchange(n, src, recv2.at[n - 2], my_c, col_peer, n_col)
        return tree(add, [recv2[n - 2, k] for k in range(n_col)]), cps

    def ref_pass(n, scale8):
        to_col(scale8)

        def step(k, ss):
            off = pl.multiple_of(k * RB, RB)
            c = colv[pl.ds(off, RB), :]
            return tuple(
                ss[q] + fold(tile[pl.ds(off, RB), q * LANES : (q + 1) * LANES] * c) for q in range(cq)
            )

        ss = lax.fori_loop(0, rows // RB, step, tuple(zero for _ in range(cq)))
        row0 = 0 if n == 3 else cq
        for q in range(cq):
            send2[pl.ds(row0 + q, 1), :] = w8[q : q + 1, :] * jnp.sum(ss[q], axis=0, keepdims=True)
        cps = exchange(n, send2.at[pl.ds(row0, cq)], recv2.at[n - 2], my_r, row_peer, n_row)
        return tree(add, [recv2[n - 2, k] for k in range(n_row)]), cps

    def drain(n, ref, count):
        all_bytes(ref, count, esend.at[n]).wait()

    drain(0, recv1g, n_col - 1)
    r, cps = gen_pass(2, w8)
    drain(1, recv1f, n_row - 1)
    c, cps = ref_pass(3, 1.0 / r)
    r, cps = gen_pass(4, w8 / c)
    for q in range(rq):
        per_q = LANES // per
        v = jnp.concatenate([gf[q * per_q + k] for k in range(per_q)], axis=0)
        v = v * v
        s = functools.reduce(add, [v[:, k * LANES : (k + 1) * LANES] for k in range(feat // LANES)])
        sqg[pl.ds(q, 1), :] = jnp.sum(s.T, axis=0, keepdims=True) * (1.0 / feat)
    g_out[...] = (gamma - jnp.log2(r)) * (1.0 / kappa) + sqg[...]
    c, cps = ref_pass(5, 1.0 / r)
    f = (phi - jnp.log2(c)) * (1.0 / kappa) + sqr[...]
    f_out[pl.ds(0, half), :] = f[:, :per]
    f_out[pl.ds(half, half), :] = f[:, per:]
    for n, count in ((2, n_col), (3, n_row), (4, n_col), (5, n_row)):
        drain(n, recv2.at[n - 2], count - 1)
    all_bytes(rf, n_row - 1, gsend.at[0]).wait()
    all_bytes(gf, n_col - 1, gsend.at[1]).wait()


def body(n_row, n_col, gx, rx, w, b, wo):
    per, vox = gx.shape
    units, feat = wo.shape
    rows, cols = per * n_col, per * n_row
    rq, cq = rows // LANES, cols // LANES
    hbm = pl.BlockSpec(memory_space=pl.ANY)
    vmem = pl.BlockSpec(memory_space=pltpu.VMEM)
    dma = pltpu.SemaphoreType.DMA
    n_chunks = max(1, vox // K_CHUNK + 1)
    g8, f2 = pl.pallas_call(
        functools.partial(kernel, n_row, n_col, math.isqrt(n_col)),
        out_shape=(jax.ShapeDtypeStruct((rq, LANES), F32), jax.ShapeDtypeStruct((n_row, per), F32)),
        in_specs=[hbm] * 5,
        out_specs=(vmem, vmem),
        scratch_shapes=[
            pltpu.VMEM((2 * per, vox), BF16),
            pltpu.VMEM((vox, units), BF16),
            pltpu.VMEM((1, units), F32),
            pltpu.VMEM((units, feat), BF16),
            pltpu.VMEM((n_col, per, feat), F32),
            pltpu.VMEM((n_row, per, feat), F32),
            pltpu.VMEM((rows, feat), BF16),
            pltpu.VMEM((rows, feat), BF16),
            pltpu.VMEM((feat, cols), BF16),
            pltpu.VMEM((feat, cols), BF16),
            pltpu.VMEM((rows, cols), F32),
            pltpu.VMEM((rows, LANES), F32),
            pltpu.VMEM((rows, LANES), F32),
            pltpu.VMEM((rows, LANES), F32),
            pltpu.VMEM((rq, LANES), F32),
            pltpu.VMEM((cq, LANES), F32),
            pltpu.VMEM((2 * rq, LANES), F32),
            pltpu.VMEM((n_col, 2 * rq, LANES), F32),
            pltpu.VMEM((n_row, 2 * cq, LANES), F32),
            pltpu.VMEM((2 * cq, LANES), F32),
            pltpu.VMEM((4, max(n_col, n_row), max(rq, cq), LANES), F32),
            dma((2,)),
            dma((n_chunks,)),
            dma((2,)),
            dma((2,)),
            dma((CHUNKS * (n_row // 2 + n_col),)),
            dma((6,)),
            dma((6,)),
        ],
        compiler_params=pltpu.CompilerParams(
            collective_id=0, has_side_effects=True, vmem_limit_bytes=60 * 1024 * 1024
        ),
    )(gx, rx, w, b.reshape(1, units), wo)
    return g8.reshape(rows), f2


def solution(mesh):
    n_row, n_col = mesh.shape["row"], mesh.shape["col"]
    return jax.shard_map(
        functools.partial(body, n_row, n_col),
        mesh=mesh,
        in_specs=(P(("row", "col"), None), P(("row", "col"), None), P(), P(), P()),
        out_specs=(P("row"), P(None, "col")),
        check_vma=False,
    )
```

```python
import functools
import math

import jax
import jax.numpy as jnp
from jax import lax
from jax.experimental import pallas as pl
from jax.experimental.pallas import tpu as pltpu
from jax.sharding import PartitionSpec as P

EPSILON = 0.1
MESH = pl.DeviceIdType.MESH
F32 = jnp.float32
BF16 = jnp.bfloat16
LANES = 128
K_CUTS = (1920, 3840, 5760)
CHUNKS = 2


def split2(v):
    hi = v.astype(BF16)
    lo = (v - hi.astype(F32)).astype(BF16)
    return hi, lo


def mm(a, b):
    return jnp.dot(a, b, preferred_element_type=F32)


def kernel(
    n_row,
    n_col,
    n_x,
    gx,
    rx,
    w,
    b,
    wo,
    g_out,
    f_out,
    x_v,
    w_v,
    b_v,
    wo_v,
    gf,
    rf,
    g_hi,
    g_lo,
    r_hi,
    r_lo,
    tile,
    part,
    part2,
    colv,
    sqg,
    sqr,
    tops,
    sums,
    send_v,
    recv,
    x_sem,
    w_sem,
    s_sem,
    gsend,
    grecv,
    esend,
    erecv,
):
    my_r = lax.axis_index("row")
    my_c = lax.axis_index("col")
    per = gx.shape[0]
    vox = gx.shape[1]
    feat = wo.shape[1]
    rows = per * n_col
    cols = per * n_row
    rq = rows // LANES
    cq = cols // LANES
    total = n_row * n_col * per
    n_y = n_col // n_x
    n_a = n_b = n_x
    kappa = 1.0 / (EPSILON * math.log(2.0))
    log2w = -math.log2(total)

    def row_peer(d):
        return (lax.rem(my_r + d, n_row), my_c)

    def col_peer(d):
        return (my_r, lax.rem(my_c + d, n_col))

    loads = [
        pltpu.make_async_copy(gx, x_v.at[pl.ds(0, per)], x_sem.at[0]),
        pltpu.make_async_copy(rx, x_v.at[pl.ds(per, per)], x_sem.at[1]),
        pltpu.make_async_copy(b, b_v, s_sem.at[0]),
        pltpu.make_async_copy(wo, wo_v, s_sem.at[1]),
    ]
    bounds = sorted({0, vox, *(k for k in K_CUTS if k < vox)})
    spans = list(zip(bounds[:-1], bounds[1:]))
    wloads = [
        pltpu.make_async_copy(w.at[pl.ds(k0, k1 - k0)], w_v.at[pl.ds(k0, k1 - k0)], w_sem.at[n])
        for n, (k0, k1) in enumerate(spans)
    ]
    loads[0].start()
    loads[1].start()
    for cp in wloads:
        cp.start()
    loads[2].start()
    loads[3].start()

    core = lax.rem(my_r, 2)
    px = my_c // n_y
    py = lax.rem(my_c, n_y)

    def z_index(d):
        return lax.rem(my_r + 2 * d + 2 * n_row, n_row)

    def partner_of(r):
        return r + 1 - 2 * core

    def ab_index(da, db):
        dx = da + (db - da) * core
        dy = db + (da - db) * core
        return lax.rem(px + dx + 2 * n_x, n_x) * n_y + lax.rem(py + dy + 2 * n_y, n_y)

    n_z = n_row // 2
    zdev = {d % n_z: (z_index(d), my_c) for d in (1, -1, 2, -2) if d % n_z}
    adev = {d % n_a: (my_r, ab_index(d, 0)) for d in (1, -1, 2) if d % n_a}
    bdev = {d % n_b: (my_r, ab_index(0, d)) for d in (1, -1, 2) if d % n_b}
    pdev = (partner_of(my_r), my_c)
    near = [*zdev.values(), *adev.values(), *bdev.values(), pdev]
    barrier = pltpu.get_barrier_semaphore()
    for dev in near:
        pl.semaphore_signal(barrier, inc=1, device_id=dev, device_id_type=MESH)

    loads[0].wait()
    loads[1].wait()
    acc = None
    for n, (k0, k1) in enumerate(spans):
        wloads[n].wait()
        t = mm(x_v[:, k0:k1], w_v[k0:k1, :])
        acc = t if acc is None else acc + t
    loads[2].wait()
    loads[3].wait()
    hidden = jnp.maximum(acc + b_v[...], 0.0)
    h0 = hidden.astype(BF16)
    h1f = hidden - h0.astype(F32)
    h1 = h1f.astype(BF16)
    h2 = (h1f - h1.astype(F32)).astype(BF16)
    wov = wo_v[...]
    feats = mm(h0, wov) + (mm(h1, wov) + mm(h2, wov))
    gf[my_c] = feats[:per]
    rf[my_r] = feats[per:]

    pl.semaphore_wait(barrier, len(near))

    ch = per // CHUNKS

    def piece(ref, block, c):
        return ref.at[block, pl.ds(c * ch, ch)]

    def send(ref, block, c, dev, slot, which):
        pltpu.make_async_remote_copy(
            piece(ref, block, c),
            piece(ref, block, c),
            gsend.at[which],
            grecv.at[slot],
            device_id=dev,
            device_id_type=MESH,
        ).start()

    def arrived(ref, block, c, slot):
        v = piece(ref, block, c)
        pltpu.make_async_copy(v, v, grecv.at[slot]).wait()

    halves = {1: range(CHUNKS // 2), -1: range(CHUNKS // 2, CHUNKS)}

    def reach(n, c):
        out = []
        for s in (1, -1):
            far = n // 2 if c in halves[s] else (n - 1) // 2
            out += [(s, h) for h in range(1, far + 1)]
        return out

    order = []
    for c in range(CHUNKS):
        for s, h in reach(n_z, c):
            order.append((h if h <= 2 else h + 3, 1 if h <= 2 else 2, c, "z", s * h, 0))
        for sb, hb in reach(n_b, c):
            order.append((hb + 2, 1, c, "b", 0, sb * hb))
        for sa, ha in reach(n_a, c):
            order.append((ha, 1, c, "a", sa * ha, 0))
            for sb, hb in reach(n_b, c):
                order.append((ha + hb + 3, 2, c, "b", sa * ha, sb * hb))
    order.sort(key=lambda o: (o[0], o[2]))
    slots = {o[2:]: n for n, o in enumerate(order)}
    last = len(slots)

    def to_z(c, block, d, step):
        send(rf, block, c, zdev[step % n_z], slots[(c, "z", d, 0)], 0)

    def to_partner(block, c):
        send(rf, block, c, pdev, last, 0)

    def to_a(c, d):
        send(gf, my_c, c, adev[d % n_a], slots[(c, "a", d, 0)], 1)

    def to_b(c, a):
        for s, h in reach(n_b, c):
            send(gf, ab_index(-a, 0), c, bdev[s * h % n_b], slots[(c, "b", a, s * h)], 1)

    for c in range(CHUNKS):
        for s, h in sorted(reach(n_z, c), key=lambda o: -o[1]):
            if h <= 2:
                to_z(c, my_r, s * h, s * h)
        for s, h in reach(n_a, c):
            to_a(c, s * h)
    for c in range(CHUNKS):
        to_b(c, 0)
        to_partner(my_r, c)
    for _, _, c, kind, p, q in order:
        slot = slots[(c, kind, p, q)]
        if kind == "z":
            block = z_index(-p)
            arrived(rf, block, c, slot)
            s = 1 if p > 0 else -1
            if p * s == 2:
                for h in (4, 3):
                    if (s, h) in reach(n_z, c):
                        to_z(c, block, s * h, s * (h - 2))
            to_partner(block, c)
        elif p and not q:
            arrived(gf, ab_index(-p, 0), c, slot)
            to_b(c, p)
        else:
            arrived(gf, ab_index(-p, -q), c, slot)

    def all_bytes(ref, count, sem):
        view = ref.at[pl.ds(0, count)]
        return pltpu.make_async_copy(view, view, sem)

    all_bytes(rf, n_z, grecv.at[last]).wait()

    scale = 2.0 * kappa / feat
    half = cq

    for q in range(rq):
        per_q = LANES // per
        v = jnp.concatenate([gf[q * per_q + k] for k in range(per_q)], axis=0)
        hi, lo = split2(v * scale)
        g_hi[pl.ds(q * LANES, LANES), :] = hi
        g_lo[pl.ds(q * LANES, LANES), :] = lo
    for q in range(cq):
        v = jnp.concatenate([rf[q], rf[q + half]], axis=0)
        vt = v.T
        sqr[pl.ds(q, 1), :] = jnp.sum(vt * vt, axis=0, keepdims=True) * (1.0 / feat)
        hi, lo = split2(vt)
        r_hi[:, pl.ds(q * LANES, LANES)] = hi
        r_lo[:, pl.ds(q * LANES, LANES)] = lo

    nt = 256

    def tile_step(n, _):
        off = pl.multiple_of(n * nt, nt)
        rh = r_hi[:, pl.ds(off, nt)]
        rl = r_lo[:, pl.ds(off, nt)]
        gh = g_hi[...]
        tile[:, pl.ds(off, nt)] = mm(gh, rh) + (mm(g_lo[...], rh) + mm(gh, rl))
        return 0

    lax.fori_loop(0, cols // nt, tile_step, 0)

    RB = 32

    def blocks(body):
        def step(n, _):
            body(pl.multiple_of(n * RB, RB))
            return 0

        lax.fori_loop(0, rows // RB, step, 0)

    def lane_groups(v):
        return [v[:, q * LANES : (q + 1) * LANES] for q in range(cq)]

    def to_dense(src, dst, op):
        for q in range(rq):
            blk = src[pl.ds(q * LANES, LANES), :].T
            dst[pl.ds(q, 1), :] = op(blk, axis=0, keepdims=True)

    def to_col(x8):
        for q in range(rq):
            colv[pl.ds(q * LANES, LANES), :] = jnp.broadcast_to(x8[q : q + 1, :], (LANES, LANES)).T

    def wide(x8, n):
        return [jnp.broadcast_to(x8[q : q + 1, :], (n, LANES)) for q in range(cq)]

    def tree(op, vs):
        vs = list(vs)
        while len(vs) > 1:
            vs = [op(vs[k], vs[k + 1]) if k + 1 < len(vs) else vs[k] for k in range(0, len(vs), 2)]
        return vs[0]

    add = lambda p, q: p + q

    def exchange(n, me, peer, count):
        recv[n, me] = send_v[n]
        for d in range(1, count):
            pltpu.make_async_remote_copy(
                send_v.at[n], recv.at[n, me], esend.at[n], erecv.at[n], device_id=peer(d), device_id_type=MESH
            ).start()
        all_bytes(recv.at[n], count - 1, erecv.at[n]).wait()
        return [recv[n, k] for k in range(count)]

    def lse2(ls):
        m = tree(jnp.maximum, ls)
        return m + jnp.log2(tree(add, [jnp.exp2(v - m) for v in ls]))

    ph = wide(-kappa * sqr[...] + log2w, RB)

    def gen_first(off):
        t = [a + p for a, p in zip(lane_groups(tile[pl.ds(off, RB), :]), ph)]
        m = tree(jnp.maximum, t)
        part[pl.ds(off, RB), :] = m
        part2[pl.ds(off, RB), :] = tree(add, [jnp.exp2(v - m) for v in t])

    blocks(gen_first)
    for q in range(rq):
        m = part[pl.ds(q * LANES, LANES), :].T
        s = part2[pl.ds(q * LANES, LANES), :].T
        top = jnp.max(m, axis=0, keepdims=True)
        tops[pl.ds(q, 1), :] = top
        sums[pl.ds(q, 1), :] = jnp.sum(s * jnp.exp2(m - top), axis=0, keepdims=True)
    send_v[0] = tops[...] + jnp.log2(sums[...])
    gamma = -lse2(exchange(0, my_c, col_peer, n_col))
    to_col(gamma + log2w)

    def col_slab(off, q):
        return tile.at[pl.ds(off, RB), pl.ds(q * LANES, LANES)]

    def fold(op, v):
        return tree(op, [v[8 * k : 8 * k + 8] for k in range(RB // 8)])

    def ref_max(n, ms):
        off = pl.multiple_of(n * RB, RB)
        c = colv[pl.ds(off, RB), :]
        return tuple(jnp.maximum(ms[q], fold(jnp.maximum, col_slab(off, q)[...] + c)) for q in range(cq))

    low = jnp.full((8, LANES), -jnp.inf, F32)
    ms = lax.fori_loop(0, rows // RB, ref_max, tuple(low for _ in range(cq)))
    for q in range(cq):
        tops[pl.ds(q, 1), :] = jnp.max(ms[q], axis=0, keepdims=True)
    cm = tops[...]
    cmb = wide(cm, RB)

    def ref_sum(n, ss):
        off = pl.multiple_of(n * RB, RB)
        c = colv[pl.ds(off, RB), :]
        out = []
        for q in range(cq):
            e = jnp.exp2(col_slab(off, q)[...] + (c - cmb[q]))
            col_slab(off, q)[...] = e
            out.append(ss[q] + fold(add, e))
        return tuple(out)

    zero = jnp.zeros((8, LANES), F32)
    ss = lax.fori_loop(0, rows // RB, ref_sum, tuple(zero for _ in range(cq)))
    for q in range(cq):
        sums[pl.ds(q, 1), :] = jnp.sum(ss[q], axis=0, keepdims=True)
    send_v[1] = cm + jnp.log2(sums[...])
    phi = -lse2(exchange(1, my_r, row_peer, n_row))
    w8 = jnp.exp2(cm + phi)

    def gen_pass(n, scale8):
        vw = wide(scale8, RB)

        def body(off):
            t = lane_groups(tile[pl.ds(off, RB), :])
            part[pl.ds(off, RB), :] = tree(add, [a * p for a, p in zip(t, vw)])

        blocks(body)
        to_dense(part, send_v.at[n], jnp.sum)
        return tree(add, exchange(n, my_c, col_peer, n_col))

    def ref_pass(n, scale8):
        to_col(scale8)

        def step(k, ss):
            off = pl.multiple_of(k * RB, RB)
            c = colv[pl.ds(off, RB), :]
            return tuple(ss[q] + fold(add, col_slab(off, q)[...] * c) for q in range(cq))

        ss = lax.fori_loop(0, rows // RB, step, tuple(zero for _ in range(cq)))
        for q in range(cq):
            sums[pl.ds(q, 1), :] = jnp.sum(ss[q], axis=0, keepdims=True)
        send_v[n] = w8 * sums[...]
        return tree(add, exchange(n, my_r, row_peer, n_row))

    r = gen_pass(2, w8)
    c = ref_pass(3, 1.0 / r)
    r = gen_pass(4, w8 / c)
    for q in range(rq):
        per_q = LANES // per
        v = jnp.concatenate([gf[q * per_q + k] for k in range(per_q)], axis=0)
        v = v * v
        s = functools.reduce(add, [v[:, k * LANES : (k + 1) * LANES] for k in range(feat // LANES)])
        sqg[pl.ds(q, 1), :] = jnp.sum(s.T, axis=0, keepdims=True) * (1.0 / feat)
    g_out[...] = (gamma - jnp.log2(r)) * (1.0 / kappa) + sqg[...]
    c = ref_pass(5, 1.0 / r)
    f = (phi - jnp.log2(c)) * (1.0 / kappa) + sqr[...]
    f_out[pl.ds(0, half), :] = f[:, :per]
    f_out[pl.ds(half, half), :] = f[:, per:]
    for n in range(6):
        all_bytes(recv.at[n], (n_row if n % 2 else n_col) - 1, esend.at[n]).wait()
    all_bytes(rf, n_row - 1, gsend.at[0]).wait()
    all_bytes(gf, n_col - 1, gsend.at[1]).wait()


def body(n_row, n_col, gx, rx, w, b, wo):
    per, vox = gx.shape
    units, feat = wo.shape
    rows, cols = per * n_col, per * n_row
    rq, cq = rows // LANES, cols // LANES
    hbm = pl.BlockSpec(memory_space=pl.ANY)
    vmem = pl.BlockSpec(memory_space=pltpu.VMEM)
    dma = pltpu.SemaphoreType.DMA
    n_chunks = len(K_CUTS) + 1
    g8, f2 = pl.pallas_call(
        functools.partial(kernel, n_row, n_col, math.isqrt(n_col)),
        out_shape=(pltpu.VMEM((rq, LANES), F32), pltpu.VMEM((n_row, per), F32)),
        in_specs=[hbm] * 5,
        out_specs=(vmem, vmem),
        scratch_shapes=[
            pltpu.VMEM((2 * per, vox), BF16),
            pltpu.VMEM((vox, units), BF16),
            pltpu.VMEM((1, units), F32),
            pltpu.VMEM((units, feat), BF16),
            pltpu.VMEM((n_col, per, feat), F32),
            pltpu.VMEM((n_row, per, feat), F32),
            pltpu.VMEM((rows, feat), BF16),
            pltpu.VMEM((rows, feat), BF16),
            pltpu.VMEM((feat, cols), BF16),
            pltpu.VMEM((feat, cols), BF16),
            pltpu.VMEM((rows, cols), F32),
            pltpu.VMEM((rows, LANES), F32),
            pltpu.VMEM((rows, LANES), F32),
            pltpu.VMEM((rows, LANES), F32),
            pltpu.VMEM((rq, LANES), F32),
            pltpu.VMEM((cq, LANES), F32),
            pltpu.VMEM((rq, LANES), F32),
            pltpu.VMEM((cq, LANES), F32),
            pltpu.VMEM((6, rq, LANES), F32),
            pltpu.VMEM((6, max(n_col, n_row), rq, LANES), F32),
            dma((2,)),
            dma((n_chunks,)),
            dma((2,)),
            dma((2,)),
            dma((CHUNKS * (n_row // 2 + n_col),)),
            dma((6,)),
            dma((6,)),
        ],
        compiler_params=pltpu.CompilerParams(
            collective_id=0, has_side_effects=True, vmem_limit_bytes=60 * 1024 * 1024
        ),
    )(gx, rx, w, b.reshape(1, units), wo)
    return g8.reshape(rows), f2


def solution(mesh):
    n_row, n_col = mesh.shape["row"], mesh.shape["col"]
    return jax.shard_map(
        functools.partial(body, n_row, n_col),
        mesh=mesh,
        in_specs=(P(("row", "col"), None), P(("row", "col"), None), P(), P(), P()),
        out_specs=(P("row"), P(None, "col")),
        check_vma=False,
    )
```

```python
import functools
import math

import jax
import jax.numpy as jnp
from jax import lax
from jax.experimental import pallas as pl
from jax.experimental.pallas import tpu as pltpu
from jax.sharding import PartitionSpec as P

EPSILON = 0.1
MESH = pl.DeviceIdType.MESH
F32 = jnp.float32
BF16 = jnp.bfloat16
LANES = 128
K_CUTS = (2176, 4352)
CHUNKS = 2


def split2(v):
    hi = v.astype(BF16)
    lo = (v - hi.astype(F32)).astype(BF16)
    return hi, lo


def mm(a, b):
    return jnp.dot(a, b, preferred_element_type=F32)


def kernel(
    n_row,
    n_col,
    n_x,
    gx,
    rx,
    w,
    b,
    wo,
    g_out,
    f_out,
    x_v,
    w_v,
    b_v,
    wo_v,
    gf,
    rf,
    g_hi,
    g_lo,
    r_hi,
    r_lo,
    tile,
    part,
    part2,
    colv,
    sqg,
    sqr,
    tops,
    sums,
    send_v,
    recv,
    x_sem,
    w_sem,
    s_sem,
    gsend,
    grecv,
    esend,
    erecv,
):
    my_r = lax.axis_index("row")
    my_c = lax.axis_index("col")
    per = gx.shape[0]
    vox = gx.shape[1]
    feat = wo.shape[1]
    rows = per * n_col
    cols = per * n_row
    rq = rows // LANES
    cq = cols // LANES
    total = n_row * n_col * per
    n_y = n_col // n_x
    n_a = n_b = n_x
    kappa = 1.0 / (EPSILON * math.log(2.0))
    log2w = -math.log2(total)

    loads = [
        pltpu.make_async_copy(gx, x_v.at[pl.ds(0, per)], x_sem.at[0]),
        pltpu.make_async_copy(rx, x_v.at[pl.ds(per, per)], x_sem.at[1]),
        pltpu.make_async_copy(b, b_v, s_sem.at[0]),
        pltpu.make_async_copy(wo, wo_v, s_sem.at[1]),
    ]
    bounds = sorted({0, vox, *(k for k in K_CUTS if k < vox)})
    spans = list(zip(bounds[:-1], bounds[1:]))
    wloads = [
        pltpu.make_async_copy(w.at[pl.ds(k0, k1 - k0)], w_v.at[pl.ds(k0, k1 - k0)], w_sem.at[n])
        for n, (k0, k1) in enumerate(spans)
    ]
    loads[0].start()
    loads[1].start()
    for cp in wloads:
        cp.start()
    loads[2].start()
    loads[3].start()

    core = lax.rem(my_r, 2)
    px = my_c // n_y
    py = lax.rem(my_c, n_y)

    def z_index(d):
        return lax.rem(my_r + 2 * d + 2 * n_row, n_row)

    def partner_of(r):
        return r + 1 - 2 * core

    def ab_index(da, db):
        dx = da + (db - da) * core
        dy = db + (da - db) * core
        return lax.rem(px + dx + 2 * n_x, n_x) * n_y + lax.rem(py + dy + 2 * n_y, n_y)

    n_z = n_row // 2
    zdev = {d % n_z: (z_index(d), my_c) for d in (1, -1, 2, -2) if d % n_z}
    adev = {d % n_a: (my_r, ab_index(d, 0)) for d in (1, -1, 2) if d % n_a}
    bdev = {d % n_b: (my_r, ab_index(0, d)) for d in (1, -1, 2) if d % n_b}
    pdev = (partner_of(my_r), my_c)
    near = [*zdev.values(), *adev.values(), *bdev.values(), pdev]
    barrier = pltpu.get_barrier_semaphore()
    for dev in near:
        pl.semaphore_signal(barrier, inc=1, device_id=dev, device_id_type=MESH)

    loads[0].wait()
    loads[1].wait()
    acc = None
    for n, (k0, k1) in enumerate(spans):
        wloads[n].wait()
        t = mm(x_v[:, k0:k1], w_v[k0:k1, :])
        acc = t if acc is None else acc + t
    loads[2].wait()
    loads[3].wait()
    hidden = jnp.maximum(acc + b_v[...], 0.0)
    h0 = hidden.astype(BF16)
    h1f = hidden - h0.astype(F32)
    h1 = h1f.astype(BF16)
    h2 = (h1f - h1.astype(F32)).astype(BF16)
    wov = wo_v[...]
    feats = mm(h0, wov) + (mm(h1, wov) + mm(h2, wov))
    gf[my_c] = feats[:per]
    rf[my_r] = feats[per:]

    pl.semaphore_wait(barrier, len(near))

    ch = per // CHUNKS

    def piece(ref, block, c):
        return ref.at[block, pl.ds(c * ch, ch)]

    def send(ref, block, c, dev, slot, which):
        pltpu.make_async_remote_copy(
            piece(ref, block, c),
            piece(ref, block, c),
            gsend.at[which],
            grecv.at[slot],
            device_id=dev,
            device_id_type=MESH,
        ).start()

    def arrived(ref, block, c, slot):
        v = piece(ref, block, c)
        pltpu.make_async_copy(v, v, grecv.at[slot]).wait()

    halves = {1: range(CHUNKS // 2), -1: range(CHUNKS // 2, CHUNKS)}

    def reach(n, c):
        out = []
        for s in (1, -1):
            far = n // 2 if c in halves[s] else (n - 1) // 2
            out += [(s, h) for h in range(1, far + 1)]
        return sorted(out, key=lambda o: -o[1])

    order = []
    for c in range(CHUNKS):
        for s, h in reach(n_z, c):
            order.append(({1: 1, 2: 0}.get(h, 2), c, c, "z", s * h, 0))
        for sb, hb in reach(n_b, c):
            order.append((3, c, c, "b", 0, sb * hb))
        for sa, ha in reach(n_a, c):
            order.append((0, c, c, "a", sa * ha, 0))
            for sb, hb in reach(n_b, c):
                order.append((4, c, c, "b", sa * ha, sb * hb))
    order.sort(key=lambda o: o[:2])
    slots = {o[2:]: n for n, o in enumerate(order)}
    last = len(slots)

    def to_z(c, block, d, step):
        send(rf, block, c, zdev[step % n_z], slots[(c, "z", d, 0)], 0)

    def to_partner(block, c):
        send(rf, block, c, pdev, last, 0)

    def to_a(c, d):
        send(gf, my_c, c, adev[d % n_a], slots[(c, "a", d, 0)], 1)

    def to_b(c, a):
        for s, h in reach(n_b, c):
            send(gf, ab_index(-a, 0), c, bdev[s * h % n_b], slots[(c, "b", a, s * h)], 1)

    for c in range(CHUNKS):
        for s, h in reach(n_z, c):
            if h == 2:
                to_z(c, my_r, s * h, s * h)
        for s, h in reach(n_a, c):
            to_a(c, s * h)
    for c in range(CHUNKS):
        for s, h in reach(n_z, c):
            if h == 1:
                to_z(c, my_r, s * h, s * h)
        to_b(c, 0)
    for c in range(CHUNKS):
        to_partner(my_r, c)
    for _, _, c, kind, p, q in order:
        slot = slots[(c, kind, p, q)]
        if kind == "z":
            block = z_index(-p)
            arrived(rf, block, c, slot)
            s = 1 if p > 0 else -1
            if p * s == 2:
                for h in (4, 3):
                    if (s, h) in reach(n_z, c):
                        to_z(c, block, s * h, s * (h - 2))
            to_partner(block, c)
        elif p and not q:
            arrived(gf, ab_index(-p, 0), c, slot)
            to_b(c, p)
        else:
            arrived(gf, ab_index(-p, -q), c, slot)

    def all_bytes(ref, count, sem):
        view = ref.at[pl.ds(0, count)]
        return pltpu.make_async_copy(view, view, sem)

    all_bytes(rf, n_z, grecv.at[last]).wait()

    scale = 2.0 * kappa / feat
    half = cq

    for q in range(rq):
        per_q = LANES // per
        v = jnp.concatenate([gf[q * per_q + k] for k in range(per_q)], axis=0)
        hi, lo = split2(v * scale)
        g_hi[pl.ds(q * LANES, LANES), :] = hi
        g_lo[pl.ds(q * LANES, LANES), :] = lo
    for q in range(cq):
        v = jnp.concatenate([rf[q], rf[q + half]], axis=0)
        vt = v.T
        sqr[pl.ds(q, 1), :] = jnp.sum(vt * vt, axis=0, keepdims=True) * (1.0 / feat)
        hi, lo = split2(vt)
        r_hi[:, pl.ds(q * LANES, LANES)] = hi
        r_lo[:, pl.ds(q * LANES, LANES)] = lo

    nt = 256

    def tile_step(n, _):
        off = pl.multiple_of(n * nt, nt)
        rh = r_hi[:, pl.ds(off, nt)]
        rl = r_lo[:, pl.ds(off, nt)]
        gh = g_hi[...]
        tile[:, pl.ds(off, nt)] = mm(gh, rh) + (mm(g_lo[...], rh) + mm(gh, rl))
        return 0

    lax.fori_loop(0, cols // nt, tile_step, 0)

    RB = 32

    def blocks(body):
        def step(n, _):
            body(pl.multiple_of(n * RB, RB))
            return 0

        lax.fori_loop(0, rows // RB, step, 0)

    def lane_groups(v):
        return [v[:, q * LANES : (q + 1) * LANES] for q in range(cq)]

    def to_dense(src, dst, op):
        for q in range(rq):
            blk = src[pl.ds(q * LANES, LANES), :].T
            dst[pl.ds(q, 1), :] = op(blk, axis=0, keepdims=True)

    def to_col(x8):
        for q in range(rq):
            colv[pl.ds(q * LANES, LANES), :] = jnp.broadcast_to(x8[q : q + 1, :], (LANES, LANES)).T

    def wide(x8, n):
        return [jnp.broadcast_to(x8[q : q + 1, :], (n, LANES)) for q in range(cq)]

    def tree(op, vs):
        vs = list(vs)
        while len(vs) > 1:
            vs = [op(vs[k], vs[k + 1]) if k + 1 < len(vs) else vs[k] for k in range(0, len(vs), 2)]
        return vs[0]

    add = lambda p, q: p + q

    def ring(n, d):
        return min(d, n - d)

    zk = [(d, k) for d in range(n_z) for k in range(2) if d or k]
    zk.sort(key=lambda o: -ring(n_z, o[0]))
    zrow = {d: z_index(d) for d in range(n_z)}
    row_peers = [(partner_of(zrow[d]) if k else zrow[d], my_c) for d, k in zk]
    xy = [(i, j) for i in range(n_a) for j in range(n_b) if i or j]
    xy.sort(key=lambda o: -ring(n_a, o[0]) - ring(n_b, o[1]))
    col_peers = [(my_r, ab_index(*o)) for o in xy]

    def exchange(n, me, peers):
        for dev in peers:
            pltpu.make_async_remote_copy(
                send_v.at[n], recv.at[n, me], esend.at[n], erecv.at[n], device_id=dev, device_id_type=MESH
            ).start()
        recv[n, me] = send_v[n]
        all_bytes(recv.at[n], len(peers), erecv.at[n]).wait()
        return [recv[n, k] for k in range(len(peers) + 1)]

    def lse2(ls):
        m = tree(jnp.maximum, ls)
        return m + jnp.log2(tree(add, [jnp.exp2(v - m) for v in ls]))

    ph = wide(-kappa * sqr[...] + log2w, RB)

    def gen_first(off):
        t = [a + p for a, p in zip(lane_groups(tile[pl.ds(off, RB), :]), ph)]
        m = tree(jnp.maximum, t)
        part[pl.ds(off, RB), :] = m
        part2[pl.ds(off, RB), :] = tree(add, [jnp.exp2(v - m) for v in t])

    blocks(gen_first)
    for q in range(rq):
        m = part[pl.ds(q * LANES, LANES), :].T
        s = part2[pl.ds(q * LANES, LANES), :].T
        top = jnp.max(m, axis=0, keepdims=True)
        tops[pl.ds(q, 1), :] = top
        sums[pl.ds(q, 1), :] = jnp.sum(s * jnp.exp2(m - top), axis=0, keepdims=True)
    send_v[0] = tops[...] + jnp.log2(sums[...])
    gamma = -lse2(exchange(0, my_c, col_peers))
    to_col(gamma + log2w)

    def col_slab(off, q):
        return tile.at[pl.ds(off, RB), pl.ds(q * LANES, LANES)]

    def fold(op, v):
        return tree(op, [v[8 * k : 8 * k + 8] for k in range(RB // 8)])

    def ref_max(n, ms):
        off = pl.multiple_of(n * RB, RB)
        c = colv[pl.ds(off, RB), :]
        return tuple(jnp.maximum(ms[q], fold(jnp.maximum, col_slab(off, q)[...] + c)) for q in range(cq))

    low = jnp.full((8, LANES), -jnp.inf, F32)
    ms = lax.fori_loop(0, rows // RB, ref_max, tuple(low for _ in range(cq)))
    for q in range(cq):
        tops[pl.ds(q, 1), :] = jnp.max(ms[q], axis=0, keepdims=True)
    cm = tops[...]
    cmb = wide(cm, RB)

    def ref_sum(n, ss):
        off = pl.multiple_of(n * RB, RB)
        c = colv[pl.ds(off, RB), :]
        out = []
        for q in range(cq):
            e = jnp.exp2(col_slab(off, q)[...] + (c - cmb[q]))
            col_slab(off, q)[...] = e
            out.append(ss[q] + fold(add, e))
        return tuple(out)

    zero = jnp.zeros((8, LANES), F32)
    ss = lax.fori_loop(0, rows // RB, ref_sum, tuple(zero for _ in range(cq)))
    for q in range(cq):
        sums[pl.ds(q, 1), :] = jnp.sum(ss[q], axis=0, keepdims=True)
    send_v[1] = cm + jnp.log2(sums[...])
    phi = -lse2(exchange(1, my_r, row_peers))
    w8 = jnp.exp2(cm + phi)

    def gen_pass(n, scale8):
        vw = wide(scale8, RB)

        def body(off):
            t = lane_groups(tile[pl.ds(off, RB), :])
            part[pl.ds(off, RB), :] = tree(add, [a * p for a, p in zip(t, vw)])

        blocks(body)
        to_dense(part, send_v.at[n], jnp.sum)
        return tree(add, exchange(n, my_c, col_peers))

    def ref_pass(n, scale8):
        to_col(scale8)

        def step(k, ss):
            off = pl.multiple_of(k * RB, RB)
            c = colv[pl.ds(off, RB), :]
            return tuple(ss[q] + fold(add, col_slab(off, q)[...] * c) for q in range(cq))

        ss = lax.fori_loop(0, rows // RB, step, tuple(zero for _ in range(cq)))
        for q in range(cq):
            sums[pl.ds(q, 1), :] = jnp.sum(ss[q], axis=0, keepdims=True)
        send_v[n] = w8 * sums[...]
        return tree(add, exchange(n, my_r, row_peers))

    r = gen_pass(2, w8)
    c = ref_pass(3, 1.0 / r)
    r = gen_pass(4, w8 / c)
    for q in range(rq):
        per_q = LANES // per
        v = jnp.concatenate([gf[q * per_q + k] for k in range(per_q)], axis=0)
        v = v * v
        s = functools.reduce(add, [v[:, k * LANES : (k + 1) * LANES] for k in range(feat // LANES)])
        sqg[pl.ds(q, 1), :] = jnp.sum(s.T, axis=0, keepdims=True) * (1.0 / feat)
    g_out[...] = (gamma - jnp.log2(r)) * (1.0 / kappa) + sqg[...]
    c = ref_pass(5, 1.0 / r)
    f = (phi - jnp.log2(c)) * (1.0 / kappa) + sqr[...]
    f_out[pl.ds(0, half), :] = f[:, :per]
    f_out[pl.ds(half, half), :] = f[:, per:]
    for n in range(6):
        all_bytes(recv.at[n], (n_row if n % 2 else n_col) - 1, esend.at[n]).wait()
    all_bytes(rf, n_row - 1, gsend.at[0]).wait()
    all_bytes(gf, n_col - 1, gsend.at[1]).wait()


def body(n_row, n_col, gx, rx, w, b, wo):
    per, vox = gx.shape
    units, feat = wo.shape
    rows, cols = per * n_col, per * n_row
    rq, cq = rows // LANES, cols // LANES
    hbm = pl.BlockSpec(memory_space=pl.ANY)
    vmem = pl.BlockSpec(memory_space=pltpu.VMEM)
    dma = pltpu.SemaphoreType.DMA
    n_chunks = len(K_CUTS) + 1
    g8, f2 = pl.pallas_call(
        functools.partial(kernel, n_row, n_col, math.isqrt(n_col)),
        out_shape=(pltpu.VMEM((rq, LANES), F32), pltpu.VMEM((n_row, per), F32)),
        in_specs=[hbm] * 5,
        out_specs=(vmem, vmem),
        scratch_shapes=[
            pltpu.VMEM((2 * per, vox), BF16),
            pltpu.VMEM((vox, units), BF16),
            pltpu.VMEM((1, units), F32),
            pltpu.VMEM((units, feat), BF16),
            pltpu.VMEM((n_col, per, feat), F32),
            pltpu.VMEM((n_row, per, feat), F32),
            pltpu.VMEM((rows, feat), BF16),
            pltpu.VMEM((rows, feat), BF16),
            pltpu.VMEM((feat, cols), BF16),
            pltpu.VMEM((feat, cols), BF16),
            pltpu.VMEM((rows, cols), F32),
            pltpu.VMEM((rows, LANES), F32),
            pltpu.VMEM((rows, LANES), F32),
            pltpu.VMEM((rows, LANES), F32),
            pltpu.VMEM((rq, LANES), F32),
            pltpu.VMEM((cq, LANES), F32),
            pltpu.VMEM((rq, LANES), F32),
            pltpu.VMEM((cq, LANES), F32),
            pltpu.VMEM((6, rq, LANES), F32),
            pltpu.VMEM((6, max(n_col, n_row), rq, LANES), F32),
            dma((2,)),
            dma((n_chunks,)),
            dma((2,)),
            dma((2,)),
            dma((CHUNKS * (n_row // 2 + n_col),)),
            dma((6,)),
            dma((6,)),
        ],
        compiler_params=pltpu.CompilerParams(
            collective_id=0, has_side_effects=True, vmem_limit_bytes=60 * 1024 * 1024
        ),
    )(gx, rx, w, b.reshape(1, units), wo)
    return g8.reshape(rows), f2


def solution(mesh):
    n_row, n_col = mesh.shape["row"], mesh.shape["col"]
    return jax.shard_map(
        functools.partial(body, n_row, n_col),
        mesh=mesh,
        in_specs=(P(("row", "col"), None), P(("row", "col"), None), P(), P(), P()),
        out_specs=(P("row"), P(None, "col")),
        check_vma=False,
    )
```

```python
import functools
import math

import jax
import jax.numpy as jnp
from jax import lax
from jax.experimental import pallas as pl
from jax.experimental.pallas import tpu as pltpu
from jax.sharding import PartitionSpec as P

EPSILON = 0.1
MESH = pl.DeviceIdType.MESH
F32 = jnp.float32
BF16 = jnp.bfloat16
LANES = 128
K_CUTS = (2176, 4352)
CHUNKS = 2
RB = 32
UNROLL = 4


def split2(v):
    hi = v.astype(BF16)
    lo = (v - hi.astype(F32)).astype(BF16)
    return hi, lo


def mm(a, b):
    return jnp.dot(a, b, preferred_element_type=F32)


def kernel(
    n_row,
    n_col,
    n_x,
    gx,
    rx,
    w,
    b,
    wo,
    g_out,
    f_out,
    x_v,
    w_v,
    b_v,
    wo_v,
    gf,
    rf,
    g_hi,
    g_lo,
    r_hi,
    r_lo,
    tile,
    part,
    part2,
    colv,
    sqg,
    sqr,
    tops,
    sums,
    send_v,
    recv,
    x_sem,
    w_sem,
    s_sem,
    gsend,
    grecv,
    esend,
    erecv,
):
    my_r = lax.axis_index("row")
    my_c = lax.axis_index("col")
    per = gx.shape[0]
    vox = gx.shape[1]
    feat = wo.shape[1]
    rows = per * n_col
    cols = per * n_row
    rq = rows // LANES
    cq = cols // LANES
    total = n_row * n_col * per
    n_y = n_col // n_x
    n_a = n_b = n_x
    kappa = 1.0 / (EPSILON * math.log(2.0))
    log2w = -math.log2(total)

    loads = [
        pltpu.make_async_copy(gx, x_v.at[pl.ds(0, per)], x_sem.at[0]),
        pltpu.make_async_copy(rx, x_v.at[pl.ds(per, per)], x_sem.at[1]),
        pltpu.make_async_copy(b, b_v, s_sem.at[0]),
        pltpu.make_async_copy(wo, wo_v, s_sem.at[1]),
    ]
    bounds = sorted({0, vox, *(k for k in K_CUTS if k < vox)})
    spans = list(zip(bounds[:-1], bounds[1:]))
    wloads = [
        pltpu.make_async_copy(w.at[pl.ds(k0, k1 - k0)], w_v.at[pl.ds(k0, k1 - k0)], w_sem.at[n])
        for n, (k0, k1) in enumerate(spans)
    ]
    loads[0].start()
    loads[1].start()
    for cp in wloads:
        cp.start()
    loads[2].start()
    loads[3].start()

    core = lax.rem(my_r, 2)
    px = my_c // n_y
    py = lax.rem(my_c, n_y)

    def z_index(d):
        return lax.rem(my_r + 2 * d + 2 * n_row, n_row)

    def partner_of(r):
        return r + 1 - 2 * core

    def ab_index(da, db):
        dx = da + (db - da) * core
        dy = db + (da - db) * core
        return lax.rem(px + dx + 2 * n_x, n_x) * n_y + lax.rem(py + dy + 2 * n_y, n_y)

    n_z = n_row // 2
    zdev = {d % n_z: (z_index(d), my_c) for d in (1, -1, 2, -2) if d % n_z}
    adev = {d % n_a: (my_r, ab_index(d, 0)) for d in (1, -1, 2) if d % n_a}
    bdev = {d % n_b: (my_r, ab_index(0, d)) for d in (1, -1, 2) if d % n_b}
    pdev = (partner_of(my_r), my_c)
    near = [*zdev.values(), *adev.values(), *bdev.values(), pdev]
    barrier = pltpu.get_barrier_semaphore()
    for dev in near:
        pl.semaphore_signal(barrier, inc=1, device_id=dev, device_id_type=MESH)

    loads[0].wait()
    loads[1].wait()
    acc = None
    for n, (k0, k1) in enumerate(spans):
        wloads[n].wait()
        t = mm(x_v[:, k0:k1], w_v[k0:k1, :])
        acc = t if acc is None else acc + t
    loads[2].wait()
    loads[3].wait()
    hidden = jnp.maximum(acc + b_v[...], 0.0)
    h0 = hidden.astype(BF16)
    h1f = hidden - h0.astype(F32)
    h1 = h1f.astype(BF16)
    h2 = (h1f - h1.astype(F32)).astype(BF16)
    wov = wo_v[...]
    feats = mm(h0, wov) + (mm(h1, wov) + mm(h2, wov))
    gf[my_c] = feats[:per]
    rf[my_r] = feats[per:]

    pl.semaphore_wait(barrier, len(near))

    ch = per // CHUNKS

    def piece(ref, block, c):
        return ref.at[block, pl.ds(c * ch, ch)]

    def send(ref, block, c, dev, slot, which):
        pltpu.make_async_remote_copy(
            piece(ref, block, c),
            piece(ref, block, c),
            gsend.at[which],
            grecv.at[slot],
            device_id=dev,
            device_id_type=MESH,
        ).start()

    def arrived(ref, block, c, slot):
        v = piece(ref, block, c)
        pltpu.make_async_copy(v, v, grecv.at[slot]).wait()

    halves = {1: range(CHUNKS // 2), -1: range(CHUNKS // 2, CHUNKS)}

    def reach(n, c):
        out = []
        for s in (1, -1):
            far = n // 2 if c in halves[s] else (n - 1) // 2
            out += [(s, h) for h in range(1, far + 1)]
        return sorted(out, key=lambda o: -o[1])

    order = []
    for c in range(CHUNKS):
        for s, h in reach(n_z, c):
            order.append(({1: 1, 2: 0}.get(h, 2), c, c, "z", s * h, 0))
        for sb, hb in reach(n_b, c):
            order.append((3, c, c, "b", 0, sb * hb))
        for sa, ha in reach(n_a, c):
            order.append((0, c, c, "a", sa * ha, 0))
            for sb, hb in reach(n_b, c):
                order.append((4, c, c, "b", sa * ha, sb * hb))
    order.sort(key=lambda o: o[:2])
    slots = {o[2:]: n for n, o in enumerate(order)}
    last = len(slots)

    def to_z(c, block, d, step):
        send(rf, block, c, zdev[step % n_z], slots[(c, "z", d, 0)], 0)

    def to_partner(block, c):
        send(rf, block, c, pdev, last, 0)

    def to_a(c, d):
        send(gf, my_c, c, adev[d % n_a], slots[(c, "a", d, 0)], 1)

    def to_b(c, a):
        for s, h in reach(n_b, c):
            send(gf, ab_index(-a, 0), c, bdev[s * h % n_b], slots[(c, "b", a, s * h)], 1)

    for c in range(CHUNKS):
        for s, h in reach(n_z, c):
            if h == 2:
                to_z(c, my_r, s * h, s * h)
        for s, h in reach(n_a, c):
            to_a(c, s * h)
    for c in range(CHUNKS):
        for s, h in reach(n_z, c):
            if h == 1:
                to_z(c, my_r, s * h, s * h)
        to_b(c, 0)
    for c in range(CHUNKS):
        to_partner(my_r, c)
    def all_bytes(ref, count, sem):
        view = ref.at[pl.ds(0, count)]
        return pltpu.make_async_copy(view, view, sem)

    def take(some):
        for level, _, c, kind, p, q in order:
            if level not in some:
                continue
            slot = slots[(c, kind, p, q)]
            if kind == "z":
                block = z_index(-p)
                arrived(rf, block, c, slot)
                s = 1 if p > 0 else -1
                if p * s == 2:
                    for h in (4, 3):
                        if (s, h) in reach(n_z, c):
                            to_z(c, block, s * h, s * (h - 2))
                to_partner(block, c)
            elif p and not q:
                arrived(gf, ab_index(-p, 0), c, slot)
                to_b(c, p)
            else:
                arrived(gf, ab_index(-p, -q), c, slot)

    scale = 2.0 * kappa / feat
    half = cq
    take((0, 1, 2, 3))
    all_bytes(rf, n_z, grecv.at[last]).wait()
    for q in range(cq):
        v = jnp.concatenate([rf[q], rf[q + half]], axis=0)
        vt = v.T
        sqr[pl.ds(q, 1), :] = jnp.sum(vt * vt, axis=0, keepdims=True) * (1.0 / feat)
        hi, lo = split2(vt)
        r_hi[:, pl.ds(q * LANES, LANES)] = hi
        r_lo[:, pl.ds(q * LANES, LANES)] = lo
    take((4,))
    for q in range(rq):
        per_q = LANES // per
        v = jnp.concatenate([gf[q * per_q + k] for k in range(per_q)], axis=0)
        hi, lo = split2(v * scale)
        g_hi[pl.ds(q * LANES, LANES), :] = hi
        g_lo[pl.ds(q * LANES, LANES), :] = lo

    nt = min(1024, cols)

    def tile_step(n, _):
        off = pl.multiple_of(n * nt, nt)
        rh = r_hi[:, pl.ds(off, nt)]
        rl = r_lo[:, pl.ds(off, nt)]
        gh = g_hi[...]
        tile[:, pl.ds(off, nt)] = mm(gh, rh) + (mm(g_lo[...], rh) + mm(gh, rl))
        return 0

    lax.fori_loop(0, cols // nt, tile_step, 0)

    def blocks(body):
        def step(n, _):
            body(pl.multiple_of(n * RB, RB))
            return 0

        lax.fori_loop(0, rows // RB, step, 0, unroll=UNROLL)

    def lane_groups(v):
        return [v[:, q * LANES : (q + 1) * LANES] for q in range(cq)]

    def to_dense(src, dst, op):
        for q in range(rq):
            blk = src[pl.ds(q * LANES, LANES), :].T
            dst[pl.ds(q, 1), :] = op(blk, axis=0, keepdims=True)

    def to_col(x8):
        for q in range(rq):
            colv[pl.ds(q * LANES, LANES), :] = jnp.broadcast_to(x8[q : q + 1, :], (LANES, LANES)).T

    def wide(x8, n):
        return [jnp.broadcast_to(x8[q : q + 1, :], (n, LANES)) for q in range(cq)]

    def tree(op, vs):
        vs = list(vs)
        while len(vs) > 1:
            vs = [op(vs[k], vs[k + 1]) if k + 1 < len(vs) else vs[k] for k in range(0, len(vs), 2)]
        return vs[0]

    add = lambda p, q: p + q

    def ring(n, d):
        return min(d, n - d)

    zk = [(d, k) for d in range(n_z) for k in range(2) if d or k]
    zk.sort(key=lambda o: -ring(n_z, o[0]))
    zrow = {d: z_index(d) for d in range(n_z)}
    row_peers = [(partner_of(zrow[d]) if k else zrow[d], my_c) for d, k in zk]
    xy = [(i, j) for i in range(n_a) for j in range(n_b) if i or j]
    xy.sort(key=lambda o: -ring(n_a, o[0]) - ring(n_b, o[1]))
    col_peers = [(my_r, ab_index(*o)) for o in xy]

    def exchange(n, me, peers):
        for dev in peers:
            pltpu.make_async_remote_copy(
                send_v.at[n], recv.at[n, me], esend.at[n], erecv.at[n], device_id=dev, device_id_type=MESH
            ).start()
        recv[n, me] = send_v[n]
        all_bytes(recv.at[n], len(peers), erecv.at[n]).wait()
        return [recv[n, k] for k in range(len(peers) + 1)]

    def lse2(ls):
        m = tree(jnp.maximum, ls)
        return m + jnp.log2(tree(add, [jnp.exp2(v - m) for v in ls]))

    ph = wide(-kappa * sqr[...] + log2w, RB)

    def gen_first(off):
        t = [a + p for a, p in zip(lane_groups(tile[pl.ds(off, RB), :]), ph)]
        m = tree(jnp.maximum, t)
        part[pl.ds(off, RB), :] = m
        part2[pl.ds(off, RB), :] = tree(add, [jnp.exp2(v - m) for v in t])

    blocks(gen_first)
    for q in range(rq):
        m = part[pl.ds(q * LANES, LANES), :].T
        s = part2[pl.ds(q * LANES, LANES), :].T
        top = jnp.max(m, axis=0, keepdims=True)
        tops[pl.ds(q, 1), :] = top
        sums[pl.ds(q, 1), :] = jnp.sum(s * jnp.exp2(m - top), axis=0, keepdims=True)
    send_v[0] = tops[...] + jnp.log2(sums[...])
    gamma = -lse2(exchange(0, my_c, col_peers))
    to_col(gamma + log2w)

    def col_slab(off, q):
        return tile.at[pl.ds(off, RB), pl.ds(q * LANES, LANES)]

    def fold(op, v):
        return tree(op, [v[8 * k : 8 * k + 8] for k in range(RB // 8)])

    def ref_max(n, ms):
        off = pl.multiple_of(n * RB, RB)
        c = colv[pl.ds(off, RB), :]
        return tuple(jnp.maximum(ms[q], fold(jnp.maximum, col_slab(off, q)[...] + c)) for q in range(cq))

    low = jnp.full((8, LANES), -jnp.inf, F32)
    ms = lax.fori_loop(0, rows // RB, ref_max, tuple(low for _ in range(cq)), unroll=UNROLL)
    for q in range(cq):
        tops[pl.ds(q, 1), :] = jnp.max(ms[q], axis=0, keepdims=True)
    cm = tops[...]
    cmb = wide(cm, RB)

    def ref_sum(n, ss):
        off = pl.multiple_of(n * RB, RB)
        c = colv[pl.ds(off, RB), :]
        out = []
        for q in range(cq):
            e = jnp.exp2(col_slab(off, q)[...] + (c - cmb[q]))
            col_slab(off, q)[...] = e
            out.append(ss[q] + fold(add, e))
        return tuple(out)

    zero = jnp.zeros((8, LANES), F32)
    ss = lax.fori_loop(0, rows // RB, ref_sum, tuple(zero for _ in range(cq)), unroll=UNROLL)
    for q in range(cq):
        sums[pl.ds(q, 1), :] = jnp.sum(ss[q], axis=0, keepdims=True)
    send_v[1] = cm + jnp.log2(sums[...])
    phi = -lse2(exchange(1, my_r, row_peers))
    w8 = jnp.exp2(cm + phi)

    def gen_pass(n, scale8):
        vw = wide(scale8, RB)

        def body(off):
            t = lane_groups(tile[pl.ds(off, RB), :])
            part[pl.ds(off, RB), :] = tree(add, [a * p for a, p in zip(t, vw)])

        blocks(body)
        to_dense(part, send_v.at[n], jnp.sum)
        return tree(add, exchange(n, my_c, col_peers))

    def ref_pass(n, scale8):
        to_col(scale8)

        def step(k, ss):
            off = pl.multiple_of(k * RB, RB)
            c = colv[pl.ds(off, RB), :]
            return tuple(ss[q] + fold(add, col_slab(off, q)[...] * c) for q in range(cq))

        ss = lax.fori_loop(0, rows // RB, step, tuple(zero for _ in range(cq)), unroll=UNROLL)
        for q in range(cq):
            sums[pl.ds(q, 1), :] = jnp.sum(ss[q], axis=0, keepdims=True)
        send_v[n] = w8 * sums[...]
        return tree(add, exchange(n, my_r, row_peers))

    r = gen_pass(2, w8)
    c = ref_pass(3, 1.0 / r)
    r = gen_pass(4, w8 / c)
    for q in range(rq):
        per_q = LANES // per
        v = jnp.concatenate([gf[q * per_q + k] for k in range(per_q)], axis=0)
        v = v * v
        s = functools.reduce(add, [v[:, k * LANES : (k + 1) * LANES] for k in range(feat // LANES)])
        sqg[pl.ds(q, 1), :] = jnp.sum(s.T, axis=0, keepdims=True) * (1.0 / feat)
    g_out[...] = (gamma - jnp.log2(r)) * (1.0 / kappa) + sqg[...]
    c = ref_pass(5, 1.0 / r)
    f = (phi - jnp.log2(c)) * (1.0 / kappa) + sqr[...]
    f_out[pl.ds(0, half), :] = f[:, :per]
    f_out[pl.ds(half, half), :] = f[:, per:]
    for n in range(6):
        all_bytes(recv.at[n], (n_row if n % 2 else n_col) - 1, esend.at[n]).wait()
    all_bytes(rf, n_row - 1, gsend.at[0]).wait()
    all_bytes(gf, n_col - 1, gsend.at[1]).wait()


def body(n_row, n_col, gx, rx, w, b, wo):
    per, vox = gx.shape
    units, feat = wo.shape
    rows, cols = per * n_col, per * n_row
    rq, cq = rows // LANES, cols // LANES
    hbm = pl.BlockSpec(memory_space=pl.ANY)
    vmem = pl.BlockSpec(memory_space=pltpu.VMEM)
    dma = pltpu.SemaphoreType.DMA
    n_chunks = len(K_CUTS) + 1
    g8, f2 = pl.pallas_call(
        functools.partial(kernel, n_row, n_col, math.isqrt(n_col)),
        out_shape=(pltpu.VMEM((rq, LANES), F32), pltpu.VMEM((n_row, per), F32)),
        in_specs=[hbm] * 5,
        out_specs=(vmem, vmem),
        scratch_shapes=[
            pltpu.VMEM((2 * per, vox), BF16),
            pltpu.VMEM((vox, units), BF16),
            pltpu.VMEM((1, units), F32),
            pltpu.VMEM((units, feat), BF16),
            pltpu.VMEM((n_col, per, feat), F32),
            pltpu.VMEM((n_row, per, feat), F32),
            pltpu.VMEM((rows, feat), BF16),
            pltpu.VMEM((rows, feat), BF16),
            pltpu.VMEM((feat, cols), BF16),
            pltpu.VMEM((feat, cols), BF16),
            pltpu.VMEM((rows, cols), F32),
            pltpu.VMEM((rows, LANES), F32),
            pltpu.VMEM((rows, LANES), F32),
            pltpu.VMEM((rows, LANES), F32),
            pltpu.VMEM((rq, LANES), F32),
            pltpu.VMEM((cq, LANES), F32),
            pltpu.VMEM((rq, LANES), F32),
            pltpu.VMEM((cq, LANES), F32),
            pltpu.VMEM((6, rq, LANES), F32),
            pltpu.VMEM((6, max(n_col, n_row), rq, LANES), F32),
            dma((2,)),
            dma((n_chunks,)),
            dma((2,)),
            dma((2,)),
            dma((CHUNKS * (n_row // 2 + n_col),)),
            dma((6,)),
            dma((6,)),
        ],
        compiler_params=pltpu.CompilerParams(
            collective_id=0, has_side_effects=True, vmem_limit_bytes=60 * 1024 * 1024
        ),
    )(gx, rx, w, b.reshape(1, units), wo)
    return g8.reshape(rows), f2


def solution(mesh):
    n_row, n_col = mesh.shape["row"], mesh.shape["col"]
    return jax.shard_map(
        functools.partial(body, n_row, n_col),
        mesh=mesh,
        in_specs=(P(("row", "col"), None), P(("row", "col"), None), P(), P(), P()),
        out_specs=(P("row"), P(None, "col")),
        check_vma=False,
    )
```

```python
import functools
import math

import jax
import jax.numpy as jnp
from jax import lax
from jax.experimental import pallas as pl
from jax.experimental.pallas import tpu as pltpu
from jax.sharding import PartitionSpec as P

EPSILON = 0.1
MESH = pl.DeviceIdType.MESH
F32 = jnp.float32
BF16 = jnp.bfloat16
LANES = 128
K_CUTS = (2176, 4352)
CHUNKS = 2
RB = 32
UNROLL = 8


def split2(v):
    hi = v.astype(BF16)
    lo = (v - hi.astype(F32)).astype(BF16)
    return hi, lo


def mm(a, b):
    return jnp.dot(a, b, preferred_element_type=F32)


def kernel(
    n_row,
    n_col,
    n_x,
    gx,
    rx,
    w,
    b,
    wo,
    g_out,
    f_out,
    x_v,
    w_v,
    b_v,
    wo_v,
    gf,
    rf,
    g_cat,
    r_cat,
    tile,
    part,
    part2,
    colv,
    sqg,
    sqr,
    tops,
    sums,
    send_v,
    recv,
    x_sem,
    w_sem,
    s_sem,
    gsend,
    grecv,
    esend,
    erecv,
):
    my_r = lax.axis_index("row")
    my_c = lax.axis_index("col")
    per = gx.shape[0]
    vox = gx.shape[1]
    feat = wo.shape[1]
    rows = per * n_col
    cols = per * n_row
    rq = rows // LANES
    cq = cols // LANES
    total = n_row * n_col * per
    n_y = n_col // n_x
    n_a = n_b = n_x
    kappa = 1.0 / (EPSILON * math.log(2.0))
    log2w = -math.log2(total)

    loads = [
        pltpu.make_async_copy(gx, x_v.at[pl.ds(0, per)], x_sem.at[0]),
        pltpu.make_async_copy(rx, x_v.at[pl.ds(per, per)], x_sem.at[1]),
        pltpu.make_async_copy(b, b_v, s_sem.at[0]),
        pltpu.make_async_copy(wo, wo_v, s_sem.at[1]),
    ]
    bounds = sorted({0, vox, *(k for k in K_CUTS if k < vox)})
    spans = list(zip(bounds[:-1], bounds[1:]))
    wloads = [
        pltpu.make_async_copy(w.at[pl.ds(k0, k1 - k0)], w_v.at[pl.ds(k0, k1 - k0)], w_sem.at[n])
        for n, (k0, k1) in enumerate(spans)
    ]
    loads[0].start()
    loads[1].start()
    for cp in wloads:
        cp.start()
    loads[2].start()
    loads[3].start()

    core = lax.rem(my_r, 2)
    px = my_c // n_y
    py = lax.rem(my_c, n_y)

    def z_index(d):
        return lax.rem(my_r + 2 * d + 2 * n_row, n_row)

    def partner_of(r):
        return r + 1 - 2 * core

    def ab_index(da, db):
        dx = da + (db - da) * core
        dy = db + (da - db) * core
        return lax.rem(px + dx + 2 * n_x, n_x) * n_y + lax.rem(py + dy + 2 * n_y, n_y)

    n_z = n_row // 2
    zdev = {d % n_z: (z_index(d), my_c) for d in (1, -1, 2, -2) if d % n_z}
    adev = {d % n_a: (my_r, ab_index(d, 0)) for d in (1, -1, 2) if d % n_a}
    bdev = {d % n_b: (my_r, ab_index(0, d)) for d in (1, -1, 2) if d % n_b}
    pdev = (partner_of(my_r), my_c)
    near = [*zdev.values(), *adev.values(), *bdev.values(), pdev]
    barrier = pltpu.get_barrier_semaphore()
    for dev in near:
        pl.semaphore_signal(barrier, inc=1, device_id=dev, device_id_type=MESH)

    loads[0].wait()
    loads[1].wait()
    acc = None
    for n, (k0, k1) in enumerate(spans):
        wloads[n].wait()
        t = mm(x_v[:, k0:k1], w_v[k0:k1, :])
        acc = t if acc is None else acc + t
    loads[2].wait()
    loads[3].wait()
    hidden = jnp.maximum(acc + b_v[...], 0.0)
    h0 = hidden.astype(BF16)
    h1f = hidden - h0.astype(F32)
    h1 = h1f.astype(BF16)
    h2 = (h1f - h1.astype(F32)).astype(BF16)
    wov = wo_v[...]
    feats = mm(h0, wov) + (mm(h1, wov) + mm(h2, wov))
    gf[my_c] = feats[:per]
    rf[my_r] = feats[per:]

    pl.semaphore_wait(barrier, len(near))

    ch = per // CHUNKS

    def piece(ref, block, c):
        return ref.at[block, pl.ds(c * ch, ch)]

    def send(ref, block, c, dev, slot, which):
        pltpu.make_async_remote_copy(
            piece(ref, block, c),
            piece(ref, block, c),
            gsend.at[which],
            grecv.at[slot],
            device_id=dev,
            device_id_type=MESH,
        ).start()

    def arrived(ref, block, c, slot):
        v = piece(ref, block, c)
        pltpu.make_async_copy(v, v, grecv.at[slot]).wait()

    halves = {1: range(CHUNKS // 2), -1: range(CHUNKS // 2, CHUNKS)}

    def reach(n, c):
        out = []
        for s in (1, -1):
            far = n // 2 if c in halves[s] else (n - 1) // 2
            out += [(s, h) for h in range(1, far + 1)]
        return sorted(out, key=lambda o: -o[1])

    order = []
    for c in range(CHUNKS):
        for s, h in reach(n_z, c):
            order.append(({1: 1, 2: 0}.get(h, 2), c, c, "z", s * h, 0))
        for sb, hb in reach(n_b, c):
            order.append((3, c, c, "b", 0, sb * hb))
        for sa, ha in reach(n_a, c):
            order.append((0, c - (ha == 1) * 0.5, c, "a", sa * ha, 0))
            for sb, hb in reach(n_b, c):
                order.append((4, c, c, "b", sa * ha, sb * hb))
    order.sort(key=lambda o: o[:2])
    slots = {o[2:]: n for n, o in enumerate(order)}
    last = len(slots)

    def to_z(c, block, d, step):
        send(rf, block, c, zdev[step % n_z], slots[(c, "z", d, 0)], 0)

    def to_partner(block, c):
        send(rf, block, c, pdev, last, 0)

    def to_a(c, d):
        send(gf, my_c, c, adev[d % n_a], slots[(c, "a", d, 0)], 1)

    def to_b(c, a):
        for s, h in reach(n_b, c):
            send(gf, ab_index(-a, 0), c, bdev[s * h % n_b], slots[(c, "b", a, s * h)], 1)

    for c in range(CHUNKS):
        for s, h in reach(n_a, c):
            to_a(c, s * h)
        for s, h in reach(n_z, c):
            if h == 2:
                to_z(c, my_r, s * h, s * h)
    for c in range(CHUNKS):
        for s, h in reach(n_z, c):
            if h == 1:
                to_z(c, my_r, s * h, s * h)
        to_b(c, 0)
    for c in range(CHUNKS):
        to_partner(my_r, c)
    def all_bytes(ref, count, sem):
        view = ref.at[pl.ds(0, count)]
        return pltpu.make_async_copy(view, view, sem)

    def take(some):
        for level, _, c, kind, p, q in order:
            if level not in some:
                continue
            slot = slots[(c, kind, p, q)]
            if kind == "z":
                block = z_index(-p)
                arrived(rf, block, c, slot)
                s = 1 if p > 0 else -1
                if p * s == 2:
                    for h in (4, 3):
                        if (s, h) in reach(n_z, c):
                            to_z(c, block, s * h, s * (h - 2))
                to_partner(block, c)
            elif p and not q:
                arrived(gf, ab_index(-p, 0), c, slot)
                to_b(c, p)
            else:
                arrived(gf, ab_index(-p, -q), c, slot)

    scale = 2.0 * kappa / feat
    half = cq
    take((0, 1, 2, 3))
    all_bytes(rf, n_z, grecv.at[last]).wait()
    for q in range(cq):
        v = jnp.concatenate([rf[q], rf[q + half]], axis=0)
        vt = v.T
        sqr[pl.ds(q, 1), :] = jnp.sum(vt * vt, axis=0, keepdims=True) * (1.0 / feat)
        hi, lo = split2(vt)
        for k, v in enumerate((hi, hi, lo)):
            r_cat[pl.ds(k * feat, feat), q * LANES : (q + 1) * LANES] = v
    take((4,))
    for q in range(rq):
        per_q = LANES // per
        v = jnp.concatenate([gf[q * per_q + k] for k in range(per_q)], axis=0)
        hi, lo = split2(v * scale)
        for k, v in enumerate((hi, lo, hi)):
            g_cat[pl.ds(q * LANES, LANES), k * feat : (k + 1) * feat] = v

    tile[...] = mm(g_cat[...], r_cat[...])

    def blocks(body):
        def step(n, _):
            body(pl.multiple_of(n * RB, RB))
            return 0

        lax.fori_loop(0, rows // RB, step, 0, unroll=UNROLL)

    def lane_groups(v):
        return [v[:, q * LANES : (q + 1) * LANES] for q in range(cq)]

    def to_dense(src, dst, op):
        for q in range(rq):
            blk = src[pl.ds(q * LANES, LANES), :].T
            dst[pl.ds(q, 1), :] = op(blk, axis=0, keepdims=True)

    def to_col(x8):
        for q in range(rq):
            colv[pl.ds(q * LANES, LANES), :] = jnp.broadcast_to(x8[q : q + 1, :], (LANES, LANES)).T

    def wide(x8, n):
        return [jnp.broadcast_to(x8[q : q + 1, :], (n, LANES)) for q in range(cq)]

    def tree(op, vs):
        vs = list(vs)
        while len(vs) > 1:
            vs = [op(vs[k], vs[k + 1]) if k + 1 < len(vs) else vs[k] for k in range(0, len(vs), 2)]
        return vs[0]

    add = lambda p, q: p + q

    def ring(n, d):
        return min(d, n - d)

    zk = [(d, k) for d in range(n_z) for k in range(2) if d or k]
    zk.sort(key=lambda o: -ring(n_z, o[0]))
    zrow = {d: z_index(d) for d in range(n_z)}
    row_peers = [(partner_of(zrow[d]) if k else zrow[d], my_c) for d, k in zk]
    xy = [(i, j) for i in range(n_a) for j in range(n_b) if i or j]
    xy.sort(key=lambda o: -ring(n_a, o[0]) - ring(n_b, o[1]))
    col_peers = [(my_r, ab_index(*o)) for o in xy]

    def exchange(n, me, peers, meanwhile=None):
        for dev in peers:
            pltpu.make_async_remote_copy(
                send_v.at[n], recv.at[n, me], esend.at[n], erecv.at[n], device_id=dev, device_id_type=MESH
            ).start()
        recv[n, me] = send_v[n]
        if meanwhile is not None:
            meanwhile()
        all_bytes(recv.at[n], len(peers), erecv.at[n]).wait()
        return [recv[n, k] for k in range(len(peers) + 1)]

    def lse2(ls):
        m = tree(jnp.maximum, ls)
        return m + jnp.log2(tree(add, [jnp.exp2(v - m) for v in ls]))

    def gen_squares():
        for q in range(rq):
            per_q = LANES // per
            v = jnp.concatenate([gf[q * per_q + k] for k in range(per_q)], axis=0)
            v = v * v
            s = functools.reduce(add, [v[:, k * LANES : (k + 1) * LANES] for k in range(feat // LANES)])
            sqg[pl.ds(q, 1), :] = jnp.sum(s.T, axis=0, keepdims=True) * (1.0 / feat)

    ph = wide(-kappa * sqr[...] + log2w, RB)

    def gen_first(off):
        t = [a + p for a, p in zip(lane_groups(tile[pl.ds(off, RB), :]), ph)]
        m = tree(jnp.maximum, t)
        part[pl.ds(off, RB), :] = m
        part2[pl.ds(off, RB), :] = tree(add, [jnp.exp2(v - m) for v in t])

    blocks(gen_first)
    for q in range(rq):
        m = part[pl.ds(q * LANES, LANES), :].T
        s = part2[pl.ds(q * LANES, LANES), :].T
        top = jnp.max(m, axis=0, keepdims=True)
        tops[pl.ds(q, 1), :] = top
        sums[pl.ds(q, 1), :] = jnp.sum(s * jnp.exp2(m - top), axis=0, keepdims=True)
    send_v[0] = tops[...] + jnp.log2(sums[...])
    gamma = -lse2(exchange(0, my_c, col_peers, gen_squares))
    to_col(gamma + log2w)

    def col_slab(off, q):
        return tile.at[pl.ds(off, RB), pl.ds(q * LANES, LANES)]

    def fold(op, v):
        return tree(op, [v[8 * k : 8 * k + 8] for k in range(RB // 8)])

    def ref_max(n, ms):
        off = pl.multiple_of(n * RB, RB)
        c = colv[pl.ds(off, RB), :]
        return tuple(jnp.maximum(ms[q], fold(jnp.maximum, col_slab(off, q)[...] + c)) for q in range(cq))

    low = jnp.full((8, LANES), -jnp.inf, F32)
    ms = lax.fori_loop(0, rows // RB, ref_max, tuple(low for _ in range(cq)), unroll=UNROLL)
    for q in range(cq):
        tops[pl.ds(q, 1), :] = jnp.max(ms[q], axis=0, keepdims=True)
    cm = tops[...]
    cmb = wide(cm, RB)

    def ref_sum(n, ss):
        off = pl.multiple_of(n * RB, RB)
        c = colv[pl.ds(off, RB), :]
        out = []
        for q in range(cq):
            e = jnp.exp2(col_slab(off, q)[...] + (c - cmb[q]))
            col_slab(off, q)[...] = e
            out.append(ss[q] + fold(add, e))
        return tuple(out)

    zero = jnp.zeros((8, LANES), F32)
    ss = lax.fori_loop(0, rows // RB, ref_sum, tuple(zero for _ in range(cq)), unroll=UNROLL)
    for q in range(cq):
        sums[pl.ds(q, 1), :] = jnp.sum(ss[q], axis=0, keepdims=True)
    send_v[1] = cm + jnp.log2(sums[...])
    phi = -lse2(exchange(1, my_r, row_peers))
    w8 = jnp.exp2(cm + phi)

    def gen_pass(n, scale8):
        vw = wide(scale8, RB)

        def body(off):
            t = lane_groups(tile[pl.ds(off, RB), :])
            part[pl.ds(off, RB), :] = tree(add, [a * p for a, p in zip(t, vw)])

        blocks(body)
        to_dense(part, send_v.at[n], jnp.sum)
        return tree(add, exchange(n, my_c, col_peers))

    def ref_pass(n, scale8, meanwhile=None):
        to_col(scale8)

        def step(k, ss):
            off = pl.multiple_of(k * RB, RB)
            c = colv[pl.ds(off, RB), :]
            return tuple(ss[q] + fold(add, col_slab(off, q)[...] * c) for q in range(cq))

        ss = lax.fori_loop(0, rows // RB, step, tuple(zero for _ in range(cq)), unroll=UNROLL)
        for q in range(cq):
            sums[pl.ds(q, 1), :] = jnp.sum(ss[q], axis=0, keepdims=True)
        send_v[n] = w8 * sums[...]
        return tree(add, exchange(n, my_r, row_peers, meanwhile))

    r = gen_pass(2, w8)
    c = ref_pass(3, 1.0 / r)
    r = gen_pass(4, w8 / c)
    def gen_result():
        g_out[...] = (gamma - jnp.log2(r)) * (1.0 / kappa) + sqg[...]
        for n in range(5):
            all_bytes(recv.at[n], (n_row if n % 2 else n_col) - 1, esend.at[n]).wait()
        all_bytes(rf, n_row - 1, gsend.at[0]).wait()
        all_bytes(gf, n_col - 1, gsend.at[1]).wait()

    c = ref_pass(5, 1.0 / r, gen_result)
    f = (phi - jnp.log2(c)) * (1.0 / kappa) + sqr[...]
    f_out[pl.ds(0, half), :] = f[:, :per]
    f_out[pl.ds(half, half), :] = f[:, per:]
    all_bytes(recv.at[5], n_row - 1, esend.at[5]).wait()


def body(n_row, n_col, gx, rx, w, b, wo):
    per, vox = gx.shape
    units, feat = wo.shape
    rows, cols = per * n_col, per * n_row
    rq, cq = rows // LANES, cols // LANES
    hbm = pl.BlockSpec(memory_space=pl.ANY)
    vmem = pl.BlockSpec(memory_space=pltpu.VMEM)
    dma = pltpu.SemaphoreType.DMA
    n_chunks = len(K_CUTS) + 1
    g8, f2 = pl.pallas_call(
        functools.partial(kernel, n_row, n_col, math.isqrt(n_col)),
        out_shape=(pltpu.VMEM((rq, LANES), F32), pltpu.VMEM((n_row, per), F32)),
        in_specs=[hbm] * 5,
        out_specs=(vmem, vmem),
        scratch_shapes=[
            pltpu.VMEM((2 * per, vox), BF16),
            pltpu.VMEM((vox, units), BF16),
            pltpu.VMEM((1, units), F32),
            pltpu.VMEM((units, feat), BF16),
            pltpu.VMEM((n_col, per, feat), F32),
            pltpu.VMEM((n_row, per, feat), F32),
            pltpu.VMEM((rows, 3 * feat), BF16),
            pltpu.VMEM((3 * feat, cols), BF16),
            pltpu.VMEM((rows, cols), F32),
            pltpu.VMEM((rows, LANES), F32),
            pltpu.VMEM((rows, LANES), F32),
            pltpu.VMEM((rows, LANES), F32),
            pltpu.VMEM((rq, LANES), F32),
            pltpu.VMEM((cq, LANES), F32),
            pltpu.VMEM((rq, LANES), F32),
            pltpu.VMEM((cq, LANES), F32),
            pltpu.VMEM((6, rq, LANES), F32),
            pltpu.VMEM((6, max(n_col, n_row), rq, LANES), F32),
            dma((2,)),
            dma((n_chunks,)),
            dma((2,)),
            dma((2,)),
            dma((CHUNKS * (n_row // 2 + n_col),)),
            dma((6,)),
            dma((6,)),
        ],
        compiler_params=pltpu.CompilerParams(
            collective_id=0, has_side_effects=True, vmem_limit_bytes=60 * 1024 * 1024
        ),
    )(gx, rx, w, b.reshape(1, units), wo)
    return g8.reshape(rows), f2


def solution(mesh):
    n_row, n_col = mesh.shape["row"], mesh.shape["col"]
    return jax.shard_map(
        functools.partial(body, n_row, n_col),
        mesh=mesh,
        in_specs=(P(("row", "col"), None), P(("row", "col"), None), P(), P(), P()),
        out_specs=(P("row"), P(None, "col")),
        check_vma=False,
    )
```

```python
import functools
import math

import jax
import jax.numpy as jnp
from jax import lax
from jax.experimental import pallas as pl
from jax.experimental.pallas import tpu as pltpu
from jax.sharding import PartitionSpec as P

EPSILON = 0.1
MESH = pl.DeviceIdType.MESH
F32 = jnp.float32
BF16 = jnp.bfloat16
LANES = 128
K_CUTS = (2176, 4352)
CHUNKS = 2
RB = 32
UNROLL = 16


def split2(v):
    hi = v.astype(BF16)
    lo = (v - hi.astype(F32)).astype(BF16)
    return hi, lo


def mm(a, b):
    return jnp.dot(a, b, preferred_element_type=F32)


def kernel(
    n_row,
    n_col,
    n_x,
    gx,
    rx,
    w,
    b,
    wo,
    g_out,
    f_out,
    x_v,
    w_v,
    b_v,
    wo_v,
    gf,
    rf,
    g_cat,
    r_cat,
    tile,
    part,
    part2,
    colv,
    sqg,
    sqr,
    tops,
    sums,
    send_v,
    recv,
    x_sem,
    w_sem,
    s_sem,
    gsend,
    grecv,
    esend,
    erecv,
):
    my_r = lax.axis_index("row")
    my_c = lax.axis_index("col")
    per = gx.shape[0]
    vox = gx.shape[1]
    feat = wo.shape[1]
    rows = per * n_col
    cols = per * n_row
    rq = rows // LANES
    cq = cols // LANES
    total = n_row * n_col * per
    n_y = n_col // n_x
    n_a = n_b = n_x
    kappa = 1.0 / (EPSILON * math.log(2.0))
    log2w = -math.log2(total)

    loads = [
        pltpu.make_async_copy(gx, x_v.at[pl.ds(0, per)], x_sem.at[0]),
        pltpu.make_async_copy(rx, x_v.at[pl.ds(per, per)], x_sem.at[1]),
        pltpu.make_async_copy(b, b_v, s_sem.at[0]),
        pltpu.make_async_copy(wo, wo_v, s_sem.at[1]),
    ]
    bounds = sorted({0, vox, *(k for k in K_CUTS if k < vox)})
    spans = list(zip(bounds[:-1], bounds[1:]))
    wloads = [
        pltpu.make_async_copy(w.at[pl.ds(k0, k1 - k0)], w_v.at[pl.ds(k0, k1 - k0)], w_sem.at[n])
        for n, (k0, k1) in enumerate(spans)
    ]
    loads[0].start()
    loads[1].start()
    for cp in wloads:
        cp.start()
    loads[2].start()
    loads[3].start()

    core = lax.rem(my_r, 2)
    px = my_c // n_y
    py = lax.rem(my_c, n_y)

    def z_index(d):
        return lax.rem(my_r + 2 * d + 2 * n_row, n_row)

    def partner_of(r):
        return r + 1 - 2 * core

    def ab_index(da, db):
        dx = da + (db - da) * core
        dy = db + (da - db) * core
        return lax.rem(px + dx + 2 * n_x, n_x) * n_y + lax.rem(py + dy + 2 * n_y, n_y)

    n_z = n_row // 2
    zdev = {d % n_z: (z_index(d), my_c) for d in (1, -1, 2, -2) if d % n_z}
    adev = {d % n_a: (my_r, ab_index(d, 0)) for d in (1, -1, 2) if d % n_a}
    bdev = {d % n_b: (my_r, ab_index(0, d)) for d in (1, -1, 2) if d % n_b}
    pdev = (partner_of(my_r), my_c)
    near = [*zdev.values(), *adev.values(), *bdev.values(), pdev]
    barrier = pltpu.get_barrier_semaphore()
    for dev in near:
        pl.semaphore_signal(barrier, inc=1, device_id=dev, device_id_type=MESH)

    loads[0].wait()
    loads[1].wait()
    acc = None
    for n, (k0, k1) in enumerate(spans):
        wloads[n].wait()
        t = mm(x_v[:, k0:k1], w_v[k0:k1, :])
        acc = t if acc is None else acc + t
    loads[2].wait()
    loads[3].wait()
    hidden = jnp.maximum(acc + b_v[...], 0.0)
    h0 = hidden.astype(BF16)
    h1f = hidden - h0.astype(F32)
    h1 = h1f.astype(BF16)
    h2 = (h1f - h1.astype(F32)).astype(BF16)
    wov = wo_v[...]
    three = mm(jnp.concatenate([h0, h1, h2], axis=0), wov)
    feats = three[: 2 * per] + (three[2 * per : 4 * per] + three[4 * per :])
    gf[my_c] = feats[:per]
    rf[my_r] = feats[per:]

    pl.semaphore_wait(barrier, len(near))

    ch = per // CHUNKS

    def piece(ref, block, c):
        return ref.at[block, pl.ds(c * ch, ch)]

    def send(ref, block, c, dev, slot, which):
        pltpu.make_async_remote_copy(
            piece(ref, block, c),
            piece(ref, block, c),
            gsend.at[which],
            grecv.at[slot],
            device_id=dev,
            device_id_type=MESH,
        ).start()

    def arrived(ref, block, c, slot):
        v = piece(ref, block, c)
        pltpu.make_async_copy(v, v, grecv.at[slot]).wait()

    halves = {1: range(CHUNKS // 2), -1: range(CHUNKS // 2, CHUNKS)}

    def reach(n, c):
        out = []
        for s in (1, -1):
            far = n // 2 if c in halves[s] else (n - 1) // 2
            out += [(s, h) for h in range(1, far + 1)]
        return sorted(out, key=lambda o: -o[1])

    order = []
    for c in range(CHUNKS):
        for s, h in reach(n_z, c):
            order.append(({1: 1, 2: 0}.get(h, 2), c, c, "z", s * h, 0))
        for sb, hb in reach(n_b, c):
            order.append((3, c, c, "b", 0, sb * hb))
        for sa, ha in reach(n_a, c):
            order.append((0, c - (ha == 1) * 0.5, c, "a", sa * ha, 0))
            for sb, hb in reach(n_b, c):
                order.append((4, c, c, "b", sa * ha, sb * hb))
    order.sort(key=lambda o: o[:2])
    slots = {o[2:]: n for n, o in enumerate(order)}
    last = len(slots)

    def to_z(c, block, d, step):
        send(rf, block, c, zdev[step % n_z], slots[(c, "z", d, 0)], 0)

    def to_partner(block, c):
        send(rf, block, c, pdev, last, 0)

    def to_a(c, d):
        send(gf, my_c, c, adev[d % n_a], slots[(c, "a", d, 0)], 1)

    def to_b(c, a):
        for s, h in reach(n_b, c):
            send(gf, ab_index(-a, 0), c, bdev[s * h % n_b], slots[(c, "b", a, s * h)], 1)

    for c in range(CHUNKS):
        for s, h in reach(n_a, c):
            to_a(c, s * h)
        for s, h in reach(n_z, c):
            if h == 2:
                to_z(c, my_r, s * h, s * h)
    for c in range(CHUNKS):
        for s, h in reach(n_z, c):
            if h == 1:
                to_z(c, my_r, s * h, s * h)
        to_b(c, 0)
    for c in range(CHUNKS):
        to_partner(my_r, c)
    def all_bytes(ref, count, sem):
        view = ref.at[pl.ds(0, count)]
        return pltpu.make_async_copy(view, view, sem)

    def take(some):
        for level, _, c, kind, p, q in order:
            if level not in some:
                continue
            slot = slots[(c, kind, p, q)]
            if kind == "z":
                block = z_index(-p)
                arrived(rf, block, c, slot)
                s = 1 if p > 0 else -1
                if p * s == 2:
                    for h in (4, 3):
                        if (s, h) in reach(n_z, c):
                            to_z(c, block, s * h, s * (h - 2))
                to_partner(block, c)
            elif p and not q:
                arrived(gf, ab_index(-p, 0), c, slot)
                to_b(c, p)
            else:
                arrived(gf, ab_index(-p, -q), c, slot)

    scale = 2.0 * kappa / feat
    half = cq
    take((0, 1, 2, 3))
    all_bytes(rf, n_z, grecv.at[last]).wait()
    for q in range(cq):
        v = jnp.concatenate([rf[q], rf[q + half]], axis=0)
        vt = v.T
        sqr[pl.ds(q, 1), :] = jnp.sum(vt * vt, axis=0, keepdims=True) * (1.0 / feat)
        hi, lo = split2(vt)
        for k, v in enumerate((hi, hi, lo)):
            r_cat[pl.ds(k * feat, feat), q * LANES : (q + 1) * LANES] = v
    take((4,))
    for q in range(rq):
        per_q = LANES // per
        v = jnp.concatenate([gf[q * per_q + k] for k in range(per_q)], axis=0)
        hi, lo = split2(v * scale)
        for k, v in enumerate((hi, lo, hi)):
            g_cat[pl.ds(q * LANES, LANES), k * feat : (k + 1) * feat] = v

    tile[...] = mm(g_cat[...], r_cat[...])

    def blocks(body):
        def step(n, _):
            body(pl.multiple_of(n * RB, RB))
            return 0

        lax.fori_loop(0, rows // RB, step, 0, unroll=UNROLL)

    def lane_groups(v):
        return [v[:, q * LANES : (q + 1) * LANES] for q in range(cq)]

    def to_dense(src, dst, op):
        for q in range(rq):
            blk = src[pl.ds(q * LANES, LANES), :].T
            dst[pl.ds(q, 1), :] = op(blk, axis=0, keepdims=True)

    def to_col(x8):
        for q in range(rq):
            colv[pl.ds(q * LANES, LANES), :] = jnp.broadcast_to(x8[q : q + 1, :], (LANES, LANES)).T

    def wide(x8, n):
        return [jnp.broadcast_to(x8[q : q + 1, :], (n, LANES)) for q in range(cq)]

    def tree(op, vs):
        vs = list(vs)
        while len(vs) > 1:
            vs = [op(vs[k], vs[k + 1]) if k + 1 < len(vs) else vs[k] for k in range(0, len(vs), 2)]
        return vs[0]

    add = lambda p, q: p + q

    def ring(n, d):
        return min(d, n - d)

    zk = [(d, k) for d in range(n_z) for k in range(2) if d or k]
    zk.sort(key=lambda o: -ring(n_z, o[0]))
    zrow = {d: z_index(d) for d in range(n_z)}
    row_peers = [(partner_of(zrow[d]) if k else zrow[d], my_c) for d, k in zk]
    xy = [(i, j) for i in range(n_a) for j in range(n_b) if i or j]
    xy.sort(key=lambda o: -ring(n_a, o[0]) - ring(n_b, o[1]))
    col_peers = [(my_r, ab_index(*o)) for o in xy]

    def exchange(n, me, peers, meanwhile=None):
        for dev in peers:
            pltpu.make_async_remote_copy(
                send_v.at[n], recv.at[n, me], esend.at[n], erecv.at[n], device_id=dev, device_id_type=MESH
            ).start()
        recv[n, me] = send_v[n]
        if meanwhile is not None:
            meanwhile()
        all_bytes(recv.at[n], len(peers), erecv.at[n]).wait()
        return [recv[n, k] for k in range(len(peers) + 1)]

    def lse2(ls):
        m = tree(jnp.maximum, ls)
        return m + jnp.log2(tree(add, [jnp.exp2(v - m) for v in ls]))

    def gen_squares():
        for q in range(rq):
            per_q = LANES // per
            v = jnp.concatenate([gf[q * per_q + k] for k in range(per_q)], axis=0)
            v = v * v
            s = functools.reduce(add, [v[:, k * LANES : (k + 1) * LANES] for k in range(feat // LANES)])
            sqg[pl.ds(q, 1), :] = jnp.sum(s.T, axis=0, keepdims=True) * (1.0 / feat)

    ph = wide(-kappa * sqr[...] + log2w, RB)

    def gen_first(off):
        t = [a + p for a, p in zip(lane_groups(tile[pl.ds(off, RB), :]), ph)]
        m = tree(jnp.maximum, t)
        part[pl.ds(off, RB), :] = m
        part2[pl.ds(off, RB), :] = tree(add, [jnp.exp2(v - m) for v in t])

    blocks(gen_first)
    for q in range(rq):
        m = part[pl.ds(q * LANES, LANES), :].T
        s = part2[pl.ds(q * LANES, LANES), :].T
        top = jnp.max(m, axis=0, keepdims=True)
        tops[pl.ds(q, 1), :] = top
        sums[pl.ds(q, 1), :] = jnp.sum(s * jnp.exp2(m - top), axis=0, keepdims=True)
    send_v[0] = tops[...] + jnp.log2(sums[...])
    gamma = -lse2(exchange(0, my_c, col_peers, gen_squares))
    to_col(gamma + log2w)

    def col_slab(off, q):
        return tile.at[pl.ds(off, RB), pl.ds(q * LANES, LANES)]

    def fold(op, v):
        return tree(op, [v[8 * k : 8 * k + 8] for k in range(RB // 8)])

    def ref_max(n, ms):
        off = pl.multiple_of(n * RB, RB)
        c = colv[pl.ds(off, RB), :]
        return tuple(jnp.maximum(ms[q], fold(jnp.maximum, col_slab(off, q)[...] + c)) for q in range(cq))

    low = jnp.full((8, LANES), -jnp.inf, F32)
    ms = lax.fori_loop(0, rows // RB, ref_max, tuple(low for _ in range(cq)), unroll=UNROLL)
    for q in range(cq):
        tops[pl.ds(q, 1), :] = jnp.max(ms[q], axis=0, keepdims=True)
    cm = tops[...]
    cmb = wide(cm, RB)

    def ref_sum(n, ss):
        off = pl.multiple_of(n * RB, RB)
        c = colv[pl.ds(off, RB), :]
        out = []
        for q in range(cq):
            e = jnp.exp2(col_slab(off, q)[...] + (c - cmb[q]))
            col_slab(off, q)[...] = e
            out.append(ss[q] + fold(add, e))
        return tuple(out)

    zero = jnp.zeros((8, LANES), F32)
    ss = lax.fori_loop(0, rows // RB, ref_sum, tuple(zero for _ in range(cq)), unroll=UNROLL)
    for q in range(cq):
        sums[pl.ds(q, 1), :] = jnp.sum(ss[q], axis=0, keepdims=True)
    send_v[1] = cm + jnp.log2(sums[...])
    phi = -lse2(exchange(1, my_r, row_peers))
    w8 = jnp.exp2(cm + phi)

    def gen_pass(n, scale8):
        vw = wide(scale8, RB)

        def body(off):
            t = lane_groups(tile[pl.ds(off, RB), :])
            part[pl.ds(off, RB), :] = tree(add, [a * p for a, p in zip(t, vw)])

        blocks(body)
        to_dense(part, send_v.at[n], jnp.sum)
        return tree(add, exchange(n, my_c, col_peers))

    def ref_pass(n, scale8, meanwhile=None):
        to_col(scale8)

        def step(k, ss):
            off = pl.multiple_of(k * RB, RB)
            c = colv[pl.ds(off, RB), :]
            return tuple(ss[q] + fold(add, col_slab(off, q)[...] * c) for q in range(cq))

        ss = lax.fori_loop(0, rows // RB, step, tuple(zero for _ in range(cq)), unroll=UNROLL)
        for q in range(cq):
            sums[pl.ds(q, 1), :] = jnp.sum(ss[q], axis=0, keepdims=True)
        send_v[n] = w8 * sums[...]
        return tree(add, exchange(n, my_r, row_peers, meanwhile))

    r = gen_pass(2, w8)
    c = ref_pass(3, 1.0 / r)
    r = gen_pass(4, w8 / c)
    def gen_result():
        g_out[...] = (gamma - jnp.log2(r)) * (1.0 / kappa) + sqg[...]
        for n in range(5):
            all_bytes(recv.at[n], (n_row if n % 2 else n_col) - 1, esend.at[n]).wait()
        all_bytes(rf, n_row - 1, gsend.at[0]).wait()
        all_bytes(gf, n_col - 1, gsend.at[1]).wait()

    c = ref_pass(5, 1.0 / r, gen_result)
    f = (phi - jnp.log2(c)) * (1.0 / kappa) + sqr[...]
    f_out[pl.ds(0, half), :] = f[:, :per]
    f_out[pl.ds(half, half), :] = f[:, per:]
    all_bytes(recv.at[5], n_row - 1, esend.at[5]).wait()


def body(n_row, n_col, gx, rx, w, b, wo):
    per, vox = gx.shape
    units, feat = wo.shape
    rows, cols = per * n_col, per * n_row
    rq, cq = rows // LANES, cols // LANES
    hbm = pl.BlockSpec(memory_space=pl.ANY)
    vmem = pl.BlockSpec(memory_space=pltpu.VMEM)
    dma = pltpu.SemaphoreType.DMA
    n_chunks = len(K_CUTS) + 1
    g8, f2 = pl.pallas_call(
        functools.partial(kernel, n_row, n_col, math.isqrt(n_col)),
        out_shape=(pltpu.VMEM((rq, LANES), F32), pltpu.VMEM((n_row, per), F32)),
        in_specs=[hbm] * 5,
        out_specs=(vmem, vmem),
        scratch_shapes=[
            pltpu.VMEM((2 * per, vox), BF16),
            pltpu.VMEM((vox, units), BF16),
            pltpu.VMEM((1, units), F32),
            pltpu.VMEM((units, feat), BF16),
            pltpu.VMEM((n_col, per, feat), F32),
            pltpu.VMEM((n_row, per, feat), F32),
            pltpu.VMEM((rows, 3 * feat), BF16),
            pltpu.VMEM((3 * feat, cols), BF16),
            pltpu.VMEM((rows, cols), F32),
            pltpu.VMEM((rows, LANES), F32),
            pltpu.VMEM((rows, LANES), F32),
            pltpu.VMEM((rows, LANES), F32),
            pltpu.VMEM((rq, LANES), F32),
            pltpu.VMEM((cq, LANES), F32),
            pltpu.VMEM((rq, LANES), F32),
            pltpu.VMEM((cq, LANES), F32),
            pltpu.VMEM((6, rq, LANES), F32),
            pltpu.VMEM((6, max(n_col, n_row), rq, LANES), F32),
            dma((2,)),
            dma((n_chunks,)),
            dma((2,)),
            dma((2,)),
            dma((CHUNKS * (n_row // 2 + n_col),)),
            dma((6,)),
            dma((6,)),
        ],
        compiler_params=pltpu.CompilerParams(
            collective_id=0, has_side_effects=True, vmem_limit_bytes=60 * 1024 * 1024
        ),
    )(gx, rx, w, b.reshape(1, units), wo)
    return g8.reshape(rows), f2


def solution(mesh):
    n_row, n_col = mesh.shape["row"], mesh.shape["col"]
    return jax.shard_map(
        functools.partial(body, n_row, n_col),
        mesh=mesh,
        in_specs=(P(("row", "col"), None), P(("row", "col"), None), P(), P(), P()),
        out_specs=(P("row"), P(None, "col")),
        check_vma=False,
    )
```
